32 devices in a mesh: slab: 8 (over z, core), grp: 4 (over y, x).
Axes of the slice: x: 2, y: 2, z: 4, core: 2. Of those that a mesh axis runs over, the one named last changes fastest.
Arguments:
- stress: bfloat16 [6, 262144], P(None, ('slab', 'grp')), may hold values from -6 to 6
- interp_weight: bfloat16 [2048, 64, 128], P(('slab', 'grp')), may hold values from -0.5 to 0.5
- block_owner: int32 [2048, 1], P(('slab', 'grp')), may hold values from 0 to 3; in each aligned block of 64 rows (0 to 63, 64 to 127, ...) at most 48 rows name the same one
- block_local: int32 [2048], P(('slab', 'grp')), may hold values from 0 to 63
- slip_system: int32 [131072], P(('slab', 'grp')), may hold values from 0 to 11
- mobility: float32 [131072], P(('slab', 'grp')), may hold values from 0.3 to 3
- position: float32 [3, 131072], P(None, ('slab', 'grp')), may hold values from -6 to 6
- target_slab: int32 [131072, 1], P(('slab', 'grp')), may hold values from 0 to 7; in each aligned block of 4096 rows (0 to 4095, 4096 to 8191, ...) at most 1024 rows name the same one
Outputs:
- distortion: float32 [6, 262144], P(None, ('slab', 'grp'))
- arrived: float32 [4, 262144], P(None, ('slab', 'grp'))
The draws below stay inside these ranges and needn't reach their ends.
Inputs may be any that keep to these rules, and one draw needn't show every extreme that they name: Among the 64 segment blocks of one device at most 48 have the same block_owner; on some device exactly 48 do. Among the 4096 segments of one device at most 1024 have the same target_slab; on some device exactly 1024 do.
All inputs are finite; a program needn't handle non-finite values.
Results may differ from the reference program's by a relative error of at most 0.01.
Values may be sent and summed in bfloat16 or wider, within the bound.
No kernel may reach another device: no remote copies, remote signals or barrier semaphores. Data moves between devices by JAX's collectives and lax.ppermute only.
A program may use at most 64 MiB of HBM per device.

```python
import math
import jax
import jax.numpy as jnp
import numpy as np
from jax import lax

NC = 6
NSYS = 12
BLK = 128
SEGB = 64
SB_DEV = 64
SEG_DEV = 4096
VBD = 64
VB_SLAB = 256
VOXELS = 262144
SEGBLOCKS = 2048
SEGS = 131072
Q = 48
CAP = 1024
SLOTS = 262144
N_SLAB = 8
N_GRP = 4


def with_ends(entries, rng, low, high):
    index_at = [jax.random.randint(jax.random.fold_in(rng, axis), (), 0, length) for axis, length in enumerate(entries.shape)]
    longest = entries.shape.index(max(entries.shape))
    neighbour = index_at[:longest] + [(index_at[longest] + 1) % entries.shape[longest]] + index_at[longest + 1:]
    return entries.at[tuple(index_at)].set(low).at[tuple(neighbour)].set(high)


def block_levels(own_key, extent, shards, smallest, largest):
    def one(dim, parts):
        heights = jax.random.uniform(jax.random.fold_in(jax.random.fold_in(own_key, 6), dim), (parts,), jnp.float32, smallest / len(shards), largest / len(shards))
        return jnp.repeat(jnp.exp(heights), extent[dim] // parts).reshape((-1,) + (1,) * (len(extent) - dim - 1))

    factor_of = one(*shards[0])
    for cut in shards[1:]:
        factor_of = factor_of * one(*cut)
    return factor_of


def deal_out(own_key, own, number, rows, amount, top, limit, slope):
    sequence = jax.random.permutation(own_key, amount)
    crowded, usual = load_shares(amount, rows * top, limit, slope, True), load_shares(amount, rows * top, limit, slope, False)
    places = jnp.arange(amount)

    def named(sizes, turn):
        used = int((sizes > 0).sum())
        fixed = max(1, used // 4)
        passed = fixed + (places - fixed + turn * (used - fixed)) % max(1, amount - fixed)
        return jnp.zeros((amount,), jnp.int32).at[sequence[jnp.where(places < fixed, places, passed)]].set(jnp.asarray(sizes, jnp.int32))

    sizes = jnp.where(number % 4 == 0, named(crowded, number // 4), named(usual, number - number // 4 - 1))
    mixed = jax.random.permutation(jax.random.fold_in(own, 3), amount)
    source_of, taker = mixed[0:amount // 2 * 2:2], mixed[1:amount // 2 * 2:2]
    room = jnp.minimum(sizes[source_of] - 1, limit - sizes[taker]) // 2
    room = jnp.where((source_of == sequence[0]) | (taker == sequence[0]) | (sizes[taker] == 0), 0, jnp.maximum(room, 0))
    passed = jax.random.randint(jax.random.fold_in(own, 4), (amount // 2,), 0, 1 << 20) % (room + 1)
    sizes = sizes.at[source_of].add(-passed).at[taker].add(passed)
    labels = jnp.searchsorted(jnp.cumsum(sizes), jnp.arange(rows * top), side="right").astype(jnp.int32)
    table = labels.reshape(top, rows).T
    table = table[jax.random.permutation(jax.random.fold_in(own, 1), rows)]
    turn = jax.random.randint(jax.random.fold_in(own, 2), (rows, 1), 0, top)
    return jnp.take_along_axis(table, (jnp.arange(top)[None, :] + turn) % top, axis=1)


def load_shares(amount, total, bound, lean, full):
    weights = [(1 << 20) // math.isqrt(standing ** lean) + 1 for standing in range(1, amount + 1)]
    largest = bound if full else min(bound, max(-(-total // amount), total * weights[0] // sum(weights)))
    least = 1 if total - largest >= amount - 1 else 0
    given, surplus = [largest] + [least] * (amount - 1), total - largest - least * (amount - 1)
    while surplus > 0:
        movable = [i for i in range(1, amount) if given[i] < largest] or [i for i in range(1, amount) if given[i] < bound]
        whole, left = sum([weights[i] for i in movable]), surplus
        for i in movable:
            addition = min(bound - given[i], max(1, left * weights[i] // whole), surplus)
            given[i] = given[i] + addition
            surplus = surplus - addition
    return np.array(given)


def noise(stream_key, shape, scale, limit, cuts=(), kind=jnp.bfloat16):
    values = scale * jax.random.normal(stream_key, shape, jnp.float32)
    if cuts:
        values = values * block_levels(stream_key, shape, cuts, -0.22, 0.18)
    return jnp.clip(values, -limit, limit).astype(kind)


def setup_inputs(seed: int = 0) -> dict:
    key_of = jax.random.split(jax.random.key(seed), 9)
    stress = noise(key_of[0], (NC, VOXELS), 1.0, 6.0, ((1, 32),))
    interp_weight = noise(key_of[1], (SEGBLOCKS, SEGB, BLK), BLK ** -0.5, 0.5, ((0, 32),))
    block_owner_keys = jax.random.split(jax.random.fold_in(key_of[2], 1), SEGBLOCKS // SB_DEV)
    block_owner_turns = jax.random.permutation(jax.random.fold_in(key_of[2], 3), SEGBLOCKS // SB_DEV)
    block_owner = jax.vmap(lambda own, number: deal_out(jax.random.fold_in(key_of[2], 2), own, number, SB_DEV, N_GRP, 1, Q, 2))(block_owner_keys, block_owner_turns).reshape((SEGBLOCKS, 1))
    block_local = with_ends(jax.random.randint(key_of[3], (SEGBLOCKS,), 0, VBD), jax.random.fold_in(key_of[3], 1), 0, VBD - 1).astype(jnp.int32)
    slip_system = with_ends(jax.random.randint(key_of[4], (SEGS,), 0, NSYS), jax.random.fold_in(key_of[4], 1), 0, NSYS - 1).astype(jnp.int32)
    mobility = jnp.clip(jnp.exp(math.log(3.0) - 2.3025851 * jax.random.uniform(key_of[5], (SEGS,), jnp.float32) ** block_levels(key_of[5], (SEGS,), ((0, 32),), -0.2, 0.2)), 0.3, 3.0)
    position = noise(key_of[6], (3, SEGS), 1.0, 6.0, ((1, 32),), jnp.float32)
    target_slab_keys = jax.random.split(jax.random.fold_in(key_of[7], 1), SEGS // SEG_DEV)
    target_slab_turns = jax.random.permutation(jax.random.fold_in(key_of[7], 3), SEGS // SEG_DEV)
    target_slab = jax.vmap(lambda own, number: deal_out(jax.random.fold_in(key_of[7], 2), own, number, SEG_DEV, N_SLAB, 1, CAP, 1))(target_slab_keys, target_slab_turns).reshape((SEGS, 1))
    return dict(stress=stress, interp_weight=interp_weight, block_owner=block_owner, block_local=block_local, slip_system=slip_system, mobility=mobility, position=position, target_slab=target_slab)


glide_time = 0.5

def slip_tables():
    normal_list = [(1.0, 1.0, 1.0), (-1.0, 1.0, 1.0), (1.0, -1.0, 1.0), (1.0, 1.0, -1.0)]
    schmid_rows = []
    glide_rows = []
    for along_x, along_y, along_z in normal_list:
        normal_vec = np.array([along_x, along_y, along_z]) / np.sqrt(3.0)
        for burgers in ((along_y, -along_x, 0.0), (along_z, 0.0, -along_x), (0.0, along_z, -along_y)):
            burgers_vec = np.array(burgers) / np.sqrt(2.0)
            tensor = 0.5 * (np.outer(normal_vec, burgers_vec) + np.outer(burgers_vec, normal_vec))
            schmid_rows.append([tensor[0, 0], tensor[1, 1], tensor[2, 2], 2.0 * tensor[1, 2], 2.0 * tensor[0, 2], 2.0 * tensor[0, 1]])
            glide_rows.append(burgers_vec)
    return (np.array(schmid_rows, np.float32).T, np.array(glide_rows, np.float32).T)

def reference(stress, interp_weight, block_owner, block_local, slip_system, mobility, position, target_slab):
    schmid_np, glide_np = slip_tables()
    schmid = jnp.asarray(schmid_np, jnp.float32)
    glide_table = jnp.asarray(glide_np, jnp.float32)
    per_slab_blocks = N_GRP * SB_DEV
    stress_slab = stress.reshape(NC, N_SLAB, VB_SLAB, BLK).transpose(1, 0, 2, 3)
    weights = interp_weight.reshape(N_SLAB, per_slab_blocks, SEGB, BLK)
    block_index = (block_owner[:, 0] * VBD + block_local).reshape(N_SLAB, per_slab_blocks).astype(jnp.int32)
    systems = slip_system.reshape(N_SLAB, per_slab_blocks, SEGB)
    mobile = mobility.reshape(N_SLAB, per_slab_blocks, SEGB)

    def per_slab(inputs):
        slab_stress, slab_weight, slab_index, slab_system, slab_mobility = inputs
        gathered = slab_stress[:, slab_index, :]
        sampled = jnp.einsum('cbv,bsv->cbs', gathered.astype(jnp.float32), slab_weight.astype(jnp.float32))
        factors = schmid[:, slab_system]
        resolved = lax.optimization_barrier(jnp.sum(factors * sampled, axis=0))
        glide_step = glide_time * slab_mobility * resolved
        weight_term = (glide_step[None] * factors).astype(jnp.bfloat16)
        spread = jnp.einsum('cbs,bsv->cbv', weight_term.astype(jnp.float32), slab_weight.astype(jnp.float32))
        dense_term = jnp.zeros((NC, VB_SLAB, BLK), jnp.float32).at[:, slab_index, :].add(spread)
        return (dense_term, glide_step)
    dense_term, glide_step = lax.map(per_slab, (stress_slab, weights, block_index, systems, mobile))
    distortion = dense_term.transpose(1, 0, 2, 3).reshape(NC, VOXELS)
    glide_flat = glide_step.reshape(SEGS)
    moved_position = position + glide_table[:, slip_system] * glide_flat[None, :]
    payload = jnp.concatenate([moved_position, glide_flat[None, :]], axis=0)
    target = target_slab[:, 0].reshape(N_SLAB, N_GRP, SEG_DEV)

    def ranks_of(row):
        onehot = (row[..., None] == jnp.arange(N_SLAB, dtype=jnp.int32)).astype(jnp.int32)
        before = jnp.cumsum(onehot, axis=1) - onehot
        return lax.optimization_barrier(jnp.sum(before * onehot, axis=2))
    slot_rank = lax.map(ranks_of, target)
    payload_rows = payload.reshape(4, N_SLAB, N_GRP, SEG_DEV)
    source = jnp.broadcast_to(jnp.arange(N_SLAB, dtype=jnp.int32)[:, None, None], target.shape)
    column = jnp.broadcast_to(jnp.arange(N_GRP, dtype=jnp.int32)[None, :, None], target.shape)
    arrived = jnp.zeros((4, N_SLAB, N_GRP, N_SLAB, CAP), jnp.float32).at[:, target, column, source, slot_rank].set(payload_rows)
    return (distortion, arrived.reshape(4, SLOTS))
```

```python
import functools

import jax
import jax.numpy as jnp
import numpy as np
from jax import lax
from jax.experimental import pallas as pl
from jax.experimental.pallas import tpu as pltpu
from jax.sharding import PartitionSpec as P

NC = 6
NSYS = 12
BLK = 128
SEGB = 64
LANES = 128
SUB = 8
PACK = 4

glide_time = 0.5

VMEM = pl.BlockSpec(memory_space=pltpu.VMEM)
SMEM = pl.BlockSpec(memory_space=pltpu.SMEM)
CONTRACT_LANES = (((1,), (1,)), ((), ()))


def slip_signs():
    normal_list = [(1, 1, 1), (-1, 1, 1), (1, -1, 1), (1, 1, -1)]
    table = np.zeros((16, 16), np.float32)
    system = 0
    for x, y, z in normal_list:
        for burgers in ((y, -x, 0), (z, 0, -x), (0, z, -y)):
            outer = np.outer((x, y, z), burgers)
            tensor = outer + outer.T
            table[:NC, system] = (
                tensor[0, 0] / 2,
                tensor[1, 1] / 2,
                tensor[2, 2] / 2,
                tensor[1, 2],
                tensor[0, 2],
                tensor[0, 1],
            )
            table[8:11, system] = burgers
            system += 1
    return table


def iota(shape, dim):
    return lax.broadcasted_iota(jnp.int32, shape, dim)


def mask(condition):
    return jnp.where(condition, 1.0, 0.0).astype(jnp.bfloat16)


def prepare_kernel(slabs, cap, table_ref, slip_ref, target_ref, factor_ref, high_ref, low_ref):
    segments = slip_ref.shape[1]
    chunks = segments // LANES
    hot = mask(iota((16, segments), 0) == slip_ref[...])
    signs = jnp.dot(table_ref[...], hot, preferred_element_type=jnp.float32)
    scale = jnp.where(iota((16, 1), 0) < 8, np.float32(1 / np.sqrt(6.0)), np.float32(1 / np.sqrt(2.0)))
    factor_ref[...] = signs * scale

    target = target_ref[...]
    upto = mask(iota((LANES, LANES), 0) <= iota((LANES, LANES), 1))
    ones = jnp.ones((LANES, LANES), jnp.bfloat16)
    before = mask(iota((chunks, chunks), 1) < iota((chunks, chunks), 0))
    slot = target * cap
    for t in range(slabs):
        here = mask(target == t)
        inside = jnp.dot(here, upto, preferred_element_type=jnp.float32)
        total = jnp.dot(here, ones, preferred_element_type=jnp.float32)
        ahead = jnp.dot(before, total.astype(jnp.bfloat16), preferred_element_type=jnp.float32)
        rank = (inside + ahead).astype(jnp.int32) - 1
        slot = slot + jnp.where(target == t, rank, 0)
    high = slot // LANES
    low = slot % LANES
    rows = slabs * cap // LANES
    for r in range(chunks):
        at = pl.ds(r * LANES, LANES)
        high_ref[:, at] = mask(iota((rows, LANES), 0) == high[r : r + 1, :])
        low_ref[:, at] = mask(iota((LANES, LANES), 0) == low[r : r + 1, :])


def glide_kernel(group, *refs):
    owner_ref, local_ref, own_ref, mobility_ref, factor_ref, weight_ref = refs[:6]
    stress_refs = refs[6 : 6 + group]
    step_ref, kept_ref = refs[6 + group : 8 + group]
    sent_refs = refs[8 + group : 7 + 2 * group]
    tiles_ref, dense_ref = refs[7 + 2 * group :]
    blocks = local_ref.shape[0]
    rows, width = stress_refs[0].shape
    per_row = width // LANES
    me = own_ref[0]
    for k in range(group):
        for t in range(per_row):
            tiles_ref[k, t, :rows, :] = stress_refs[k][:, t * LANES : (t + 1) * LANES].astype(jnp.float32)
            tiles_ref[k, t, rows:, :] = jnp.zeros((tiles_ref.shape[2] - rows, LANES), jnp.float32)
    dense_ref[...] = jnp.zeros_like(dense_ref)

    span = PACK * SEGB
    part = iota((SUB, span), 1) // SEGB
    for g in range(blocks // PACK):
        places = []
        for j in range(PACK):
            local = local_ref[g * PACK + j]
            places.append((owner_ref[g * PACK + j] ^ me, local % per_row, pl.ds(local // per_row, SUB, stride=SUB)))
        stress = jnp.concatenate([tiles_ref[a, b, c, :] for a, b, c in places], axis=0).astype(jnp.bfloat16)
        at = pl.ds(g * span, span)
        weight = weight_ref[at, :]
        crossed = lax.dot_general(stress, weight, CONTRACT_LANES, preferred_element_type=jnp.float32)
        sampled = jnp.where(part == 0, crossed[:SUB], 0.0)
        for j in range(1, PACK):
            sampled = jnp.where(part == j, crossed[j * SUB : (j + 1) * SUB], sampled)
        factors = factor_ref[:SUB, at]
        resolved = jnp.sum(factors * sampled, axis=0, keepdims=True)
        step = glide_time * mobility_ref[:, at] * resolved
        step_ref[:, at] = step
        term = step * factors
        term = jnp.concatenate([jnp.where(part == j, term, 0.0) for j in range(PACK)], axis=0).astype(jnp.bfloat16)
        spread = jnp.dot(term, weight, preferred_element_type=jnp.float32)
        for j, (a, b, c) in enumerate(places):
            dense_ref[a, b, c, :] = dense_ref[a, b, c, :] + spread[j * SUB : (j + 1) * SUB]

    for t in range(per_row):
        kept_ref[:, t * LANES : (t + 1) * LANES] = dense_ref[0, t, :rows, :]
        for k in range(1, group):
            sent_refs[k - 1][:, t * LANES : (t + 1) * LANES] = dense_ref[k, t, :rows, :].astype(jnp.bfloat16)


def route_kernel(slabs, step_ref, position_ref, factor_ref, high_ref, low_ref, out_ref, code_ref, slot_ref, move_ref):
    step = step_ref[...]
    high = high_ref[...]
    rows = high.shape[0]
    deep = rows // slabs
    for c in range(4):
        value = step if c == 3 else position_ref[c : c + 1, :] + factor_ref[8 + c : 9 + c, :] * step
        code_ref[c * rows : (c + 1) * rows, :] = high * value.astype(jnp.bfloat16)
    slot_ref[...] = lax.dot_general(code_ref[...], low_ref[...], CONTRACT_LANES, preferred_element_type=jnp.float32)
    for t in range(slabs):
        for c in range(4):
            move_ref[(t * 4 + c) * deep : (t * 4 + c + 1) * deep, :] = slot_ref[c * rows + t * deep : c * rows + (t + 1) * deep, :]
    out_ref[...] = move_ref[...].astype(jnp.bfloat16)


def finish_kernel(group, slabs, *refs):
    kept_ref = refs[0]
    got_refs = refs[1:group]
    moved_ref = refs[group]
    distortion_ref, arrived_ref = refs[group + 1 : group + 3]
    sum_ref, slot_ref = refs[group + 3 :]
    per_row = kept_ref.shape[1] // LANES
    for t in range(per_row):
        at = slice(t * LANES, (t + 1) * LANES)
        total = kept_ref[:, at]
        for ref in got_refs:
            total = total + ref[:, at].astype(jnp.float32)
        sum_ref[t] = total
    deep_rows = kept_ref.shape[0] // NC
    for b in range(deep_rows):
        for t in range(per_row):
            lane = (b * per_row + t) * LANES
            distortion_ref[:, lane : lane + LANES] = sum_ref[t, pl.ds(b, NC, stride=deep_rows), :]
    slot_ref[...] = moved_ref[...].astype(jnp.float32)
    rows = moved_ref.shape[0] // slabs
    deep = rows // 4
    for s in range(slabs):
        for b in range(deep):
            lane = (s * deep + b) * LANES
            arrived_ref[:, lane : lane + LANES] = slot_ref[pl.ds(s * rows + b, 4, stride=deep), :]


def body(
    stress, interp_weight, block_owner, block_local, slip_system, mobility, position, target_slab
):
    group = lax.axis_size("grp")
    slabs = lax.axis_size("slab")
    segments = slip_system.shape[0]
    voxels = stress.shape[1]
    cap = 2 * segments // slabs
    slot_rows = slabs * cap // LANES
    f32, bf16 = jnp.float32, jnp.bfloat16
    shape = jax.ShapeDtypeStruct
    params = pltpu.CompilerParams(vmem_limit_bytes=48 * 1024 * 1024)

    def swap(x, k):
        return lax.ppermute(x, "grp", [(i, i ^ k) for i in range(group)])

    peers = sorted(range(1, group), key=lambda k: -bin(k).count("1"))
    packed = stress.reshape(NC * SUB, voxels // SUB)
    parts = {k: swap(packed, k) for k in peers}
    parts[0] = packed

    factor, high, low = pl.pallas_call(
        functools.partial(prepare_kernel, slabs, cap),
        out_shape=(
            shape((16, segments), f32),
            shape((slot_rows, segments), bf16),
            shape((LANES, segments), bf16),
        ),
        in_specs=[VMEM] * 3,
        out_specs=[VMEM] * 3,
        compiler_params=params,
        name="prepare",
    )(
        jnp.asarray(slip_signs(), bf16),
        slip_system.reshape(1, segments),
        target_slab.reshape(segments // LANES, LANES),
    )

    me = lax.axis_index("grp").astype(jnp.int32).reshape(1)
    tile_shape = (group, voxels // SUB // LANES, SUB * SUB, LANES)
    step, kept, *sent = pl.pallas_call(
        functools.partial(glide_kernel, group),
        out_shape=(shape((1, segments), f32), shape(packed.shape, f32))
        + (shape(packed.shape, bf16),) * (group - 1),
        in_specs=[SMEM] * 3 + [VMEM] * (3 + group),
        out_specs=[VMEM] * (group + 1),
        scratch_shapes=[pltpu.VMEM(tile_shape, f32), pltpu.VMEM(tile_shape, f32)],
        compiler_params=params,
        name="glide",
    )(
        block_owner.reshape(-1),
        block_local,
        me,
        mobility.reshape(1, segments),
        factor,
        interp_weight.reshape(segments, BLK),
        *[parts[k] for k in range(group)],
    )
    got = [swap(sent[k - 1], k) for k in peers]

    moves = pl.pallas_call(
        functools.partial(route_kernel, slabs),
        out_shape=shape((4 * slot_rows, LANES), bf16),
        in_specs=[VMEM] * 5,
        out_specs=VMEM,
        scratch_shapes=[
            pltpu.VMEM((4 * slot_rows, segments), bf16),
            pltpu.VMEM((4 * slot_rows, LANES), f32),
            pltpu.VMEM((4 * slot_rows, LANES), f32),
        ],
        compiler_params=params,
        name="route",
    )(step, position, factor, high, low)
    moved = lax.all_to_all(moves, "slab", split_axis=0, concat_axis=0, tiled=True)

    return pl.pallas_call(
        functools.partial(finish_kernel, group, slabs),
        out_shape=(shape((NC, voxels), f32), shape((4, slabs * cap), f32)),
        in_specs=[VMEM] * (group + 1),
        out_specs=[VMEM] * 2,
        scratch_shapes=[
            pltpu.VMEM((voxels // SUB // LANES, NC * SUB, LANES), f32),
            pltpu.VMEM((4 * slot_rows, LANES), f32),
        ],
        compiler_params=params,
        name="finish",
    )(kept, *got, moved)


def solution(mesh):
    placed = (
        P(None, ("slab", "grp")),
        P(("slab", "grp"), None, None),
        P(("slab", "grp"), None),
        P(("slab", "grp")),
        P(("slab", "grp")),
        P(("slab", "grp")),
        P(None, ("slab", "grp")),
        P(("slab", "grp"), None),
    )
    return jax.shard_map(
        body,
        mesh=mesh,
        in_specs=placed,
        out_specs=(P(None, ("slab", "grp")), P(None, ("slab", "grp"))),
        check_vma=False,
    )
```

```python
import functools

import jax
import jax.numpy as jnp
import numpy as np
from jax import lax
from jax.experimental import pallas as pl
from jax.experimental.pallas import tpu as pltpu
from jax.sharding import PartitionSpec as P

NC = 6
NSYS = 12
BLK = 128
SEGB = 64
LANES = 128
SUB = 8
PACK = 4

glide_time = 0.5

VMEM = pl.BlockSpec(memory_space=pltpu.VMEM)
SMEM = pl.BlockSpec(memory_space=pltpu.SMEM)
HBM = pl.BlockSpec(memory_space=pl.ANY)
CONTRACT_LANES = (((1,), (1,)), ((), ()))


def slip_signs():
    normal_list = [(1, 1, 1), (-1, 1, 1), (1, -1, 1), (1, 1, -1)]
    table = np.zeros((16, 16), np.float32)
    system = 0
    for x, y, z in normal_list:
        for burgers in ((y, -x, 0), (z, 0, -x), (0, z, -y)):
            outer = np.outer((x, y, z), burgers)
            tensor = outer + outer.T
            table[:NC, system] = (
                tensor[0, 0] / 2,
                tensor[1, 1] / 2,
                tensor[2, 2] / 2,
                tensor[1, 2],
                tensor[0, 2],
                tensor[0, 1],
            )
            table[8:11, system] = burgers
            system += 1
    return table


def iota(shape, dim):
    return lax.broadcasted_iota(jnp.int32, shape, dim)


def mask(condition):
    return jnp.where(condition, 1.0, 0.0).astype(jnp.bfloat16)


def prepare_kernel(slabs, cap, table_ref, slip_ref, target_ref, source_ref, factor_ref, high_ref, low_ref, weight_ref, sem):
    fetch = pltpu.make_async_copy(source_ref, weight_ref, sem)
    fetch.start()
    segments = slip_ref.shape[1]
    chunks = segments // LANES
    hot = mask(iota((16, segments), 0) == slip_ref[...])
    signs = jnp.dot(table_ref[...], hot, preferred_element_type=jnp.float32)
    scale = jnp.where(iota((16, 1), 0) < 8, np.float32(1 / np.sqrt(6.0)), np.float32(1 / np.sqrt(2.0)))
    factor_ref[...] = signs * scale

    target = target_ref[...] ^ lax.axis_index("slab")
    upto = mask(iota((LANES, LANES), 0) <= iota((LANES, LANES), 1))
    ones = jnp.ones((LANES, LANES), jnp.bfloat16)
    before = mask(iota((chunks, chunks), 1) < iota((chunks, chunks), 0))
    slot = target * cap
    for t in range(slabs):
        here = mask(target == t)
        inside = jnp.dot(here, upto, preferred_element_type=jnp.float32)
        total = jnp.dot(here, ones, preferred_element_type=jnp.float32)
        ahead = jnp.dot(before, total.astype(jnp.bfloat16), preferred_element_type=jnp.float32)
        rank = (inside + ahead).astype(jnp.int32) - 1
        slot = slot + jnp.where(target == t, rank, 0)
    high = slot // LANES
    low = slot % LANES
    rows = slabs * cap // LANES
    for r in range(chunks):
        at = pl.ds(r * LANES, LANES)
        high_ref[:, at] = mask(iota((rows, LANES), 0) == high[r : r + 1, :])
        low_ref[:, at] = mask(iota((LANES, LANES), 0) == low[r : r + 1, :])
    fetch.wait()


def place_of(place_ref, per_row, j):
    spot = place_ref[j]
    return spot // (SUB * per_row), spot % per_row, spot // per_row % SUB


def glide_kernel(group, slabs, *refs):
    place_ref, mobility_ref, position_ref, factor_ref, high_ref, low_ref, weight_ref = refs[:7]
    stress_refs = refs[7 : 7 + group]
    term_ref = refs[7 + group]
    move_refs = refs[8 + group : 9 + group + slabs // 2]
    tiles_ref, step_ref, code_ref, slot_ref, move_ref = refs[9 + group + slabs // 2 :]
    blocks = place_ref.shape[0]
    rows, width = stress_refs[0].shape
    per_row = width // LANES
    for k in range(group):
        for t in range(per_row):
            tiles_ref[k, t, :rows, :] = stress_refs[k][:, t * LANES : (t + 1) * LANES].astype(jnp.float32)

    span = PACK * SEGB
    part = iota((SUB, span), 1) // SEGB
    real = iota((SUB, span), 0) < NC
    for g in range(blocks // PACK):
        tiles = []
        for j in range(PACK):
            a, b, c = place_of(place_ref, per_row, g * PACK + j)
            tiles.append(tiles_ref[a, b, pl.ds(c, SUB, stride=SUB), :])
        stress = jnp.concatenate(tiles, axis=0).astype(jnp.bfloat16)
        at = pl.ds(g * span, span)
        crossed = lax.dot_general(stress, weight_ref[at, :], CONTRACT_LANES, preferred_element_type=jnp.float32)
        sampled = crossed[:SUB]
        for j in range(1, PACK):
            sampled = jnp.where(part == j, crossed[j * SUB : (j + 1) * SUB], sampled)
        factors = factor_ref[:SUB, at]
        resolved = jnp.sum(jnp.where(real, factors * sampled, 0.0), axis=0, keepdims=True)
        step = glide_time * mobility_ref[:, at] * resolved
        step_ref[:, at] = step
        term_ref[:, at] = step * factors

    step = step_ref[...]
    high = high_ref[...]
    slot_rows = high.shape[0]
    deep = slot_rows // slabs
    for c in range(4):
        value = step if c == 3 else position_ref[c : c + 1, :] + factor_ref[8 + c : 9 + c, :] * step
        code_ref[c * slot_rows : (c + 1) * slot_rows, :] = high * value.astype(jnp.bfloat16)
    slot_ref[...] = lax.dot_general(code_ref[...], low_ref[...], CONTRACT_LANES, preferred_element_type=jnp.float32)
    for t in range(slabs):
        for c in range(4):
            source = c * slot_rows + t * deep
            move_ref[(t * 4 + c) * deep : (t * 4 + c + 1) * deep, :] = slot_ref[source : source + deep, :]
    sizes = [1, 1] + [2] * (slabs // 2 - 1)
    start = 0
    for ref, size in zip(move_refs, sizes):
        stop = start + size * 4 * deep
        ref[...] = move_ref[start:stop, :].astype(ref.dtype)
        start = stop


def spread_kernel(group, *refs):
    place_ref, term_ref, weight_ref, kept_ref = refs[:4]
    sent_refs = refs[4 : 3 + group]
    dense_ref, spread_ref = refs[3 + group :]
    blocks = place_ref.shape[0]
    rows, width = kept_ref.shape
    per_row = width // LANES
    span = PACK * SEGB
    part = iota((SUB, span), 1) // SEGB
    dense_ref[...] = jnp.zeros_like(dense_ref)
    for g in range(blocks // PACK):
        at = pl.ds(g * span, span)
        term = term_ref[:, at]
        term = jnp.concatenate([jnp.where(part == j, term, 0.0) for j in range(PACK)], axis=0).astype(jnp.bfloat16)
        spread_ref[g * PACK * SUB : (g + 1) * PACK * SUB, :] = jnp.dot(term, weight_ref[at, :], preferred_element_type=jnp.float32)
    for j in range(blocks):
        a, b, c = place_of(place_ref, per_row, j)
        at = pl.ds(c, NC, stride=SUB)
        dense_ref[a, b, at, :] = dense_ref[a, b, at, :] + spread_ref[j * SUB : j * SUB + NC, :]
    for t in range(per_row):
        kept_ref[:, t * LANES : (t + 1) * LANES] = dense_ref[0, t]
        for k in range(1, group):
            sent_refs[k - 1][:, t * LANES : (t + 1) * LANES] = dense_ref[k, t].astype(jnp.bfloat16)


def finish_kernel(group, slabs, *refs):
    kept_ref = refs[0]
    got_refs = refs[1:group]
    own_ref, near_ref, across_ref = refs[group : group + 3]
    far_refs = refs[group + 3 : group + 2 + slabs // 2]
    distortion_ref, arrived_ref, sum_ref, slot_ref = refs[group + 2 + slabs // 2 :]
    per_row = kept_ref.shape[1] // LANES
    for t in range(per_row):
        at = slice(t * LANES, (t + 1) * LANES)
        total = kept_ref[:, at]
        for ref in got_refs:
            total = total + ref[:, at].astype(jnp.float32)
        sum_ref[t] = total
    deep_rows = kept_ref.shape[0] // NC
    for b in range(deep_rows):
        for t in range(per_row):
            lane = (b * per_row + t) * LANES
            distortion_ref[:, lane : lane + LANES] = sum_ref[t, pl.ds(b, NC, stride=deep_rows), :]
    rows = own_ref.shape[0]
    deep = rows // 4
    slot_ref[0] = own_ref[...].astype(jnp.float32)
    slot_ref[1] = near_ref[...].astype(jnp.float32)
    for k, ref in enumerate(far_refs):
        slot_ref[2 * k + 2] = ref[:rows, :].astype(jnp.float32)
        slot_ref[2 * k + 3] = across_ref[k * rows : (k + 1) * rows, :].astype(jnp.float32)
    me = lax.axis_index("slab")
    for s in range(slabs):
        for b in range(deep):
            lane = (s * deep + b) * LANES
            arrived_ref[:, lane : lane + LANES] = slot_ref[me ^ s, pl.ds(b, 4, stride=deep), :]


def body(
    stress, interp_weight, block_owner, block_local, slip_system, mobility, position, target_slab
):
    group = lax.axis_size("grp")
    slabs = lax.axis_size("slab")
    segments = slip_system.shape[0]
    voxels = stress.shape[1]
    cap = 2 * segments // slabs
    slot_rows = slabs * cap // LANES
    f32, bf16 = jnp.float32, jnp.bfloat16
    shape = jax.ShapeDtypeStruct
    params = pltpu.CompilerParams(vmem_limit_bytes=48 * 1024 * 1024)

    def swap(x, k):
        return lax.ppermute(x, "grp", [(i, i ^ k) for i in range(group)])

    peers = sorted(range(1, group), key=lambda k: -bin(k).count("1"))
    packed = stress.reshape(NC * SUB, voxels // SUB)
    parts = {k: swap(packed, k) for k in peers}
    parts[0] = packed

    factor, high, low, weight = pl.pallas_call(
        functools.partial(prepare_kernel, slabs, cap),
        out_shape=(
            shape((16, segments), f32),
            shape((slot_rows, segments), bf16),
            shape((LANES, segments), bf16),
            shape((segments, BLK), bf16),
        ),
        in_specs=[VMEM] * 3 + [HBM],
        out_specs=[VMEM] * 4,
        scratch_shapes=[pltpu.SemaphoreType.DMA],
        compiler_params=params,
        name="prepare",
    )(
        jnp.asarray(slip_signs(), bf16),
        slip_system.reshape(1, segments),
        target_slab.reshape(segments // LANES, LANES),
        interp_weight.reshape(segments, BLK),
    )

    me = lax.axis_index("grp").astype(jnp.int32)
    place = (block_owner.reshape(-1) ^ me) * (voxels // BLK) + block_local
    tile_shape = (group, voxels // SUB // LANES, SUB * SUB, LANES)
    chunk = 4 * slot_rows // slabs
    term, own, near, *far = pl.pallas_call(
        functools.partial(glide_kernel, group, slabs),
        out_shape=(shape((SUB, segments), f32), shape((chunk, LANES), bf16), shape((chunk, LANES), bf16))
        + (shape((2 * chunk, LANES), bf16),) * (slabs // 2 - 1),
        in_specs=[SMEM] + [VMEM] * (6 + group),
        out_specs=[VMEM] * (2 + slabs // 2),
        scratch_shapes=[
            pltpu.VMEM(tile_shape, f32),
            pltpu.VMEM((1, segments), f32),
            pltpu.VMEM((4 * slot_rows, segments), bf16),
            pltpu.VMEM((4 * slot_rows, LANES), f32),
            pltpu.VMEM((4 * slot_rows, LANES), f32),
        ],
        compiler_params=params,
        name="glide",
    )(
        place,
        mobility.reshape(1, segments),
        position,
        factor,
        high,
        low,
        weight,
        *[parts[k] for k in range(group)],
    )

    def hop(x, k):
        return lax.ppermute(x, "slab", [(i, i ^ k) for i in range(slabs)])

    far = [hop(x, 2 * k + 2) for k, x in enumerate(far)]
    near = hop(near, 1)

    kept, *sent = pl.pallas_call(
        functools.partial(spread_kernel, group),
        out_shape=(shape(packed.shape, f32),) + (shape(packed.shape, bf16),) * (group - 1),
        in_specs=[SMEM] + [VMEM] * 2,
        out_specs=[VMEM] * group,
        scratch_shapes=[
            pltpu.VMEM((group, voxels // SUB // LANES, NC * SUB, LANES), f32),
            pltpu.VMEM((segments // SEGB * SUB, LANES), f32),
        ],
        compiler_params=params,
        name="spread",
    )(place, term, weight)
    got = [swap(sent[k - 1], k) for k in peers]
    across = hop(jnp.concatenate([x[chunk:] for x in far], axis=0), 1)

    return pl.pallas_call(
        functools.partial(finish_kernel, group, slabs),
        out_shape=(shape((NC, voxels), f32), shape((4, slabs * cap), f32)),
        in_specs=[VMEM] * (group + 2 + slabs // 2),
        out_specs=[VMEM] * 2,
        scratch_shapes=[
            pltpu.VMEM((voxels // SUB // LANES, NC * SUB, LANES), f32),
            pltpu.VMEM((slabs, chunk, LANES), f32),
        ],
        compiler_params=params,
        name="finish",
    )(kept, *got, own, near, across, *far)


def solution(mesh):
    placed = (
        P(None, ("slab", "grp")),
        P(("slab", "grp"), None, None),
        P(("slab", "grp"), None),
        P(("slab", "grp")),
        P(("slab", "grp")),
        P(("slab", "grp")),
        P(None, ("slab", "grp")),
        P(("slab", "grp"), None),
    )
    return jax.shard_map(
        body,
        mesh=mesh,
        in_specs=placed,
        out_specs=(P(None, ("slab", "grp")), P(None, ("slab", "grp"))),
        check_vma=False,
    )
```

```python
import functools

import jax
import jax.numpy as jnp
import numpy as np
from jax import lax
from jax.experimental import pallas as pl
from jax.experimental.pallas import tpu as pltpu
from jax.sharding import PartitionSpec as P

NC = 6
NR = 5
NSYS = 12
BLK = 128
SEGB = 64
LANES = 128
SUB = 8
PACK = 4
FIELD = 1 << 16

glide_time = 0.5

VMEM = pl.BlockSpec(memory_space=pltpu.VMEM)
SMEM = pl.BlockSpec(memory_space=pltpu.SMEM)
HBM = pl.BlockSpec(memory_space=pltpu.HBM)
CONTRACT_LANES = (((1,), (1,)), ((), ()))


def slip_signs():
    normal_list = [(1, 1, 1), (-1, 1, 1), (1, -1, 1), (1, 1, -1)]
    table = np.zeros((16, 16), np.int32)
    system = 0
    for x, y, z in normal_list:
        for burgers in ((y, -x, 0), (z, 0, -x), (0, z, -y)):
            outer = np.outer((x, y, z), burgers)
            tensor = outer + outer.T
            table[:NR, system] = (tensor[0, 0] // 2, tensor[1, 1] // 2, tensor[1, 2], tensor[0, 2], tensor[0, 1])
            table[8:11, system] = burgers
            system += 1
    return table


def iota(shape, dim):
    return lax.broadcasted_iota(jnp.int32, shape, dim)


def mask(condition):
    return jnp.where(condition, 1.0, 0.0).astype(jnp.bfloat16)


def pack_kernel(source_ref, owner_ref, local_ref, packed_ref, place_ref, stress_ref, rows_ref, block_ref, sems):
    copies = [
        pltpu.make_async_copy(source_ref, stress_ref, sems.at[0]),
        pltpu.make_async_copy(owner_ref, block_ref.at[0], sems.at[1]),
        pltpu.make_async_copy(local_ref, block_ref.at[1], sems.at[2]),
    ]
    for copy in copies:
        copy.start()
    for copy in copies:
        copy.wait()
    local = block_ref[1]
    place_ref[...] = (block_ref[0] ^ lax.axis_index("grp")) * FIELD + local // SUB * (NR * SUB) + local % SUB
    for block in range(stress_ref.shape[1] // LANES):
        stress = stress_ref[:, block * LANES : (block + 1) * LANES].astype(jnp.float32)
        row = block // SUB * NR * SUB + block % SUB
        rows_ref[pl.ds(row, 2, stride=SUB), :] = stress[:2] - stress[2:3]
        rows_ref[pl.ds(row + 2 * SUB, 3, stride=SUB), :] = stress[3:]
    packed_ref[...] = rows_ref[...].astype(jnp.bfloat16)


def prepare_kernel(slabs, cap, slip_ref, target_ref, source_ref, factor_ref, high_ref, low_ref, weight_ref, sem):
    fetch = pltpu.make_async_copy(source_ref, weight_ref, sem)
    fetch.start()
    segments = slip_ref.shape[1]
    chunks = segments // LANES
    hot = mask(iota((16, segments), 0) == slip_ref[...])
    spot = iota((16, 16), 0) * 16 + iota((16, 16), 1)
    table = jnp.zeros((16, 16), jnp.float32)
    for (row, system), sign in np.ndenumerate(slip_signs()):
        if sign:
            table = jnp.where(spot == row * 16 + system, float(sign), table)
    signs = jnp.dot(table.astype(jnp.bfloat16), hot, preferred_element_type=jnp.float32)
    scale = jnp.where(iota((16, 1), 0) < 8, np.float32(1 / np.sqrt(6.0)), np.float32(1 / np.sqrt(2.0)))
    factor_ref[...] = signs * scale

    target = target_ref[...] ^ lax.axis_index("slab")
    upto = mask(iota((LANES, LANES), 0) <= iota((LANES, LANES), 1))
    ones = jnp.ones((LANES, LANES), jnp.bfloat16)
    before = mask(iota((chunks, chunks), 1) < iota((chunks, chunks), 0))
    slot = target * cap
    for t in range(slabs):
        here = mask(target == t)
        inside = jnp.dot(here, upto, preferred_element_type=jnp.float32)
        total = jnp.dot(here, ones, preferred_element_type=jnp.float32)
        ahead = jnp.dot(before, total.astype(jnp.bfloat16), preferred_element_type=jnp.float32)
        rank = (inside + ahead).astype(jnp.int32) - 1
        slot = slot + jnp.where(target == t, rank, 0)
    high = slot // LANES
    low = slot % LANES
    rows = slabs * cap // LANES
    for r in range(chunks):
        at = pl.ds(r * LANES, LANES)
        high_ref[:, at] = mask(iota((rows, LANES), 0) == high[r : r + 1, :])
        low_ref[:, at] = mask(iota((LANES, LANES), 0) == low[r : r + 1, :])
    fetch.wait()


def glide_kernel(group, slabs, *refs):
    place_ref, mobility_ref, position_ref, factor_ref, high_ref, low_ref, weight_ref = refs[:7]
    stress_refs = refs[7 : 7 + group]
    term_ref = refs[7 + group]
    keep_ref, send_ref = refs[8 + group : 10 + group]
    tiles_ref, step_ref, code_ref, slot_ref, move_ref = refs[10 + group :]
    blocks = place_ref.shape[0]
    rows = stress_refs[0].shape[0]
    for k in range(group):
        tiles_ref[k, :rows, :] = stress_refs[k][...].astype(jnp.float32)

    span = PACK * SEGB
    part = iota((SUB, span), 1) // SEGB
    real = iota((SUB, span), 0) < NR
    for g in range(blocks // PACK):
        tiles = []
        for j in range(PACK):
            spot = place_ref[g * PACK + j]
            tiles.append(tiles_ref[spot // FIELD, pl.ds(spot % FIELD, SUB, stride=SUB), :])
        stress = jnp.concatenate(tiles, axis=0).astype(jnp.bfloat16)
        at = pl.ds(g * span, span)
        crossed = lax.dot_general(stress, weight_ref[at, :], CONTRACT_LANES, preferred_element_type=jnp.float32)
        sampled = crossed[:SUB]
        for j in range(1, PACK):
            sampled = jnp.where(part == j, crossed[j * SUB : (j + 1) * SUB], sampled)
        factors = factor_ref[:SUB, at]
        resolved = jnp.sum(jnp.where(real, factors * sampled, 0.0), axis=0, keepdims=True)
        step = glide_time * mobility_ref[:, at] * resolved
        step_ref[:, at] = step
        term_ref[:, at] = step * factors

    step = step_ref[...]
    high = high_ref[...]
    slot_rows = high.shape[0]
    deep = slot_rows // slabs
    for c in range(4):
        value = step if c == 3 else position_ref[c : c + 1, :] + factor_ref[8 + c : 9 + c, :] * step
        code_ref[c * slot_rows : (c + 1) * slot_rows, :] = high * value.astype(jnp.bfloat16)
    slot_ref[...] = lax.dot_general(code_ref[...], low_ref[...], CONTRACT_LANES, preferred_element_type=jnp.float32)
    for t in range(slabs):
        for c in range(4):
            source = c * slot_rows + t * deep
            move_ref[(t * 4 + c) * deep : (t * 4 + c + 1) * deep, :] = slot_ref[source : source + deep, :]
    half = keep_ref.shape[0]
    keep_ref[...] = move_ref[:half, :].astype(keep_ref.dtype)
    send_ref[...] = move_ref[half:, :].astype(send_ref.dtype)


def spread_kernel(group, *refs):
    place_ref, term_ref, weight_ref, kept_ref = refs[:4]
    sent_refs = refs[4 : 3 + group]
    dense_ref, spread_ref = refs[3 + group :]
    blocks = place_ref.shape[0]
    span = PACK * SEGB
    part = iota((SUB, span), 1) // SEGB
    dense_ref[...] = jnp.zeros_like(dense_ref)
    for g in range(blocks // PACK):
        at = pl.ds(g * span, span)
        term = term_ref[:, at]
        term = jnp.concatenate([jnp.where(part == j, term, 0.0) for j in range(PACK)], axis=0).astype(jnp.bfloat16)
        spread_ref[g * PACK * SUB : (g + 1) * PACK * SUB, :] = jnp.dot(term, weight_ref[at, :], preferred_element_type=jnp.float32)
    for j in range(blocks):
        spot = place_ref[j]
        at = pl.ds(spot % FIELD, NR, stride=SUB)
        dense_ref[spot // FIELD, at, :] = dense_ref[spot // FIELD, at, :] + spread_ref[j * SUB : j * SUB + NR, :]
    kept_ref[...] = dense_ref[0]
    for k in range(1, group):
        sent_refs[k - 1][...] = dense_ref[k].astype(jnp.bfloat16)


def gather_kernel(chunk, picks, *refs):
    for k, (which, place) in enumerate(picks):
        refs[-1][k * chunk : (k + 1) * chunk, :] = refs[which][place * chunk : (place + 1) * chunk, :]


def finish_kernel(group, slabs, picks, *refs):
    kept_ref = refs[0]
    got_refs = refs[1:group]
    moved_refs = refs[group:-4]
    distortion_ref, arrived_ref, sum_ref, slot_ref = refs[-4:]
    total = kept_ref[...]
    for ref in got_refs:
        total = total + ref[...].astype(jnp.float32)
    sum_ref[...] = total
    for block in range(distortion_ref.shape[1] // LANES):
        row = block // SUB * NR * SUB + block % SUB
        part = sum_ref[pl.ds(row, NR, stride=SUB), :]
        at = slice(block * LANES, (block + 1) * LANES)
        distortion_ref[:2, at] = part[:2]
        distortion_ref[2:3, at] = -(part[:1] + part[1:2])
        distortion_ref[3:, at] = part[2:]
    rows = slot_ref.shape[1]
    deep = rows // 4
    for source, (which, place) in picks.items():
        slot_ref[source] = moved_refs[which][place * rows : (place + 1) * rows, :].astype(jnp.float32)
    me = lax.axis_index("slab")
    for s in range(slabs):
        for b in range(deep):
            lane = (s * deep + b) * LANES
            arrived_ref[:, lane : lane + LANES] = slot_ref[me ^ s, pl.ds(b, 4, stride=deep), :]


def body(
    stress, interp_weight, block_owner, block_local, slip_system, mobility, position, target_slab
):
    group = lax.axis_size("grp")
    slabs = lax.axis_size("slab")
    segments = slip_system.shape[0]
    voxels = stress.shape[1]
    cap = 2 * segments // slabs
    slot_rows = slabs * cap // LANES
    f32, bf16 = jnp.float32, jnp.bfloat16
    shape = jax.ShapeDtypeStruct
    params = pltpu.CompilerParams(vmem_limit_bytes=48 * 1024 * 1024)

    def swap(x, k):
        return lax.ppermute(x, "grp", [(i, i ^ k) for i in range(group)])

    peers = sorted(range(1, group), key=lambda k: -bin(k).count("1"))
    blocks = block_local.shape[0]

    def still(x):
        return pltpu.with_memory_space_constraint(x, pltpu.HBM)

    packed, place = pl.pallas_call(
        pack_kernel,
        out_shape=(shape((NR * voxels // LANES, LANES), bf16), shape((1, blocks), jnp.int32)),
        in_specs=[HBM] * 3,
        out_specs=[VMEM] * 2,
        scratch_shapes=[
            pltpu.VMEM(stress.shape, bf16),
            pltpu.VMEM((NR * voxels // LANES, LANES), f32),
            pltpu.VMEM((2, 1, blocks), jnp.int32),
            pltpu.SemaphoreType.DMA((3,)),
        ],
        compiler_params=params,
        name="pack",
    )(still(stress), still(block_owner.reshape(1, blocks)), still(block_local.reshape(1, blocks)))
    place = place.reshape(blocks)
    parts = {k: swap(packed, k) for k in peers}
    parts[0] = packed

    factor, high, low, weight = pl.pallas_call(
        functools.partial(prepare_kernel, slabs, cap),
        out_shape=(
            shape((16, segments), f32),
            shape((slot_rows, segments), bf16),
            shape((LANES, segments), bf16),
            shape((segments, BLK), bf16),
        ),
        in_specs=[VMEM] * 2 + [HBM],
        out_specs=[VMEM] * 4,
        scratch_shapes=[pltpu.SemaphoreType.DMA],
        compiler_params=params,
        name="prepare",
    )(
        slip_system.reshape(1, segments),
        target_slab.reshape(segments // LANES, LANES),
        still(interp_weight.reshape(segments, BLK)),
    )

    tile_shape = (group, packed.shape[0] + (SUB - NR) * SUB, LANES)
    chunk = 4 * slot_rows // slabs
    term, keep, send = pl.pallas_call(
        functools.partial(glide_kernel, group, slabs),
        out_shape=(shape((SUB, segments), f32),) + (shape((slabs // 2 * chunk, LANES), bf16),) * 2,
        in_specs=[SMEM] + [VMEM] * (6 + group),
        out_specs=[VMEM] * 3,
        scratch_shapes=[
            pltpu.VMEM(tile_shape, f32),
            pltpu.VMEM((1, segments), f32),
            pltpu.VMEM((4 * slot_rows, segments), bf16),
            pltpu.VMEM((4 * slot_rows, LANES), f32),
            pltpu.VMEM((4 * slot_rows, LANES), f32),
        ],
        compiler_params=params,
        name="glide",
    )(
        place,
        mobility.reshape(1, segments),
        position,
        factor,
        high,
        low,
        weight,
        *[parts[k] for k in range(group)],
    )

    def hop(x, k):
        return lax.ppermute(x, "slab", [(i, i ^ k) for i in range(slabs)])

    bit = slabs // 2
    arrays = [keep, hop(send, bit)]
    held = {(r, s * bit): (s, r) for r in range(bit) for s in range(2)}
    while bit > 1:
        bit //= 2
        leaving = {key: at for key, at in sorted(held.items(), key=lambda item: item[0][::-1]) if key[0] & bit}
        send = pl.pallas_call(
            functools.partial(gather_kernel, chunk, tuple(leaving.values())),
            out_shape=shape((len(leaving) * chunk, LANES), bf16),
            in_specs=[VMEM] * len(arrays),
            out_specs=VMEM,
            compiler_params=params,
            name="gather",
        )(*arrays)
        for k, key in enumerate(leaving):
            del held[key]
            held[key[0] ^ bit, key[1] | bit] = (len(arrays), k)
        arrays.append(hop(send, bit))

    kept, *sent = pl.pallas_call(
        functools.partial(spread_kernel, group),
        out_shape=(shape(packed.shape, f32),) + (shape(packed.shape, bf16),) * (group - 1),
        in_specs=[SMEM] + [VMEM] * 2,
        out_specs=[VMEM] * group,
        scratch_shapes=[
            pltpu.VMEM((group,) + packed.shape, f32),
            pltpu.VMEM((segments // SEGB * SUB, LANES), f32),
        ],
        compiler_params=params,
        name="spread",
    )(place, term, weight)
    got = [swap(sent[k - 1], k) for k in peers]
    return pl.pallas_call(
        functools.partial(finish_kernel, group, slabs, {s: at for (_, s), at in held.items()}),
        out_shape=(shape((NC, voxels), f32), shape((4, slabs * cap), f32)),
        in_specs=[VMEM] * (group + len(arrays)),
        out_specs=[VMEM] * 2,
        scratch_shapes=[
            pltpu.VMEM(packed.shape, f32),
            pltpu.VMEM((slabs, chunk, LANES), f32),
        ],
        compiler_params=params,
        name="finish",
    )(kept, *got, *arrays)


def solution(mesh):
    placed = (
        P(None, ("slab", "grp")),
        P(("slab", "grp"), None, None),
        P(("slab", "grp"), None),
        P(("slab", "grp")),
        P(("slab", "grp")),
        P(("slab", "grp")),
        P(None, ("slab", "grp")),
        P(("slab", "grp"), None),
    )
    return jax.shard_map(
        body,
        mesh=mesh,
        in_specs=placed,
        out_specs=(P(None, ("slab", "grp")), P(None, ("slab", "grp"))),
        check_vma=False,
    )
```

```python
import functools

import jax
import jax.numpy as jnp
import numpy as np
from jax import lax
from jax.experimental import pallas as pl
from jax.experimental.pallas import tpu as pltpu
from jax.sharding import PartitionSpec as P

NC = 6
NR = 5
NSYS = 12
BLK = 128
SEGB = 64
LANES = 128
SUB = 8
PACK = 4

glide_time = 0.5

VMEM = pl.BlockSpec(memory_space=pltpu.VMEM)
HBM = pl.BlockSpec(memory_space=pltpu.HBM)
CONTRACT_LANES = (((1,), (1,)), ((), ()))


def slip_signs():
    normal_list = [(1, 1, 1), (-1, 1, 1), (1, -1, 1), (1, 1, -1)]
    table = np.zeros((16, 16), np.int32)
    system = 0
    for x, y, z in normal_list:
        for burgers in ((y, -x, 0), (z, 0, -x), (0, z, -y)):
            outer = np.outer((x, y, z), burgers)
            tensor = outer + outer.T
            table[:NR, system] = (tensor[0, 0] // 2, tensor[1, 1] // 2, tensor[1, 2], tensor[0, 2], tensor[0, 1])
            table[8:11, system] = burgers
            system += 1
    return table


def iota(shape, dim):
    return lax.broadcasted_iota(jnp.int32, shape, dim)


def mask(condition):
    return jnp.where(condition, 1.0, 0.0).astype(jnp.bfloat16)


def pack_kernel(source_ref, owner_ref, local_ref, packed_ref, place_ref, stress_ref, rows_ref, block_ref, sems):
    copies = [
        pltpu.make_async_copy(source_ref, stress_ref, sems.at[0]),
        pltpu.make_async_copy(owner_ref, block_ref.at[0], sems.at[1]),
        pltpu.make_async_copy(local_ref, block_ref.at[1], sems.at[2]),
    ]
    for copy in copies:
        copy.start()
    for copy in copies:
        copy.wait()
    blocks = stress_ref.shape[1] // LANES
    place_ref[...] = (block_ref[0] ^ lax.axis_index("grp")) * blocks + block_ref[1]
    for block in range(blocks):
        stress = stress_ref[:, block * LANES : (block + 1) * LANES].astype(jnp.float32)
        rows_ref[pl.ds(block, 2, stride=blocks), :] = stress[:2] - stress[2:3]
        rows_ref[pl.ds(block + 2 * blocks, 3, stride=blocks), :] = stress[3:]
    packed_ref[...] = rows_ref[...].astype(jnp.bfloat16)


def prepare_kernel(slabs, cap, *refs):
    slip_ref, target_ref, place_ref, position_ref, source_ref = refs[:5]
    factor_ref, high_ref, low_ref, pick_ref, put_ref, start_ref, course_ref, weight_ref = refs[5:13]
    code_ref, sem = refs[13:]
    fetch = pltpu.make_async_copy(source_ref, weight_ref, sem)
    fetch.start()
    segments = slip_ref.shape[1]
    chunks = segments // LANES
    hot = mask(iota((16, segments), 0) == slip_ref[...])
    spot = iota((16, 16), 0) * 16 + iota((16, 16), 1)
    table = jnp.zeros((16, 16), jnp.float32)
    for (row, system), sign in np.ndenumerate(slip_signs()):
        if sign:
            table = jnp.where(spot == row * 16 + system, float(sign), table)
    signs = jnp.dot(table.astype(jnp.bfloat16), hot, preferred_element_type=jnp.float32)
    scale = jnp.where(iota((16, 1), 0) < 8, np.float32(1 / np.sqrt(6.0)), np.float32(1 / np.sqrt(2.0)))
    factors = signs * scale
    factor_ref[...] = factors[:SUB]
    blocks, choices = pick_ref.shape
    place = jnp.concatenate([place_ref[...], place_ref[...]], axis=1)
    put = jnp.where(iota((choices, 2 * blocks), 0) == place, 1.0, 0.0)
    put_ref[...] = put.astype(jnp.bfloat16)
    pick_ref[...] = put.T[:blocks].astype(jnp.bfloat16)

    target = target_ref[...] ^ lax.axis_index("slab")
    upto = mask(iota((LANES, LANES), 0) <= iota((LANES, LANES), 1))
    ones = jnp.ones((LANES, LANES), jnp.bfloat16)
    before = mask(iota((chunks, chunks), 1) < iota((chunks, chunks), 0))
    slot = target * cap
    for t in range(slabs):
        here = mask(target == t)
        inside = jnp.dot(here, upto, preferred_element_type=jnp.float32)
        total = jnp.dot(here, ones, preferred_element_type=jnp.float32)
        ahead = jnp.dot(before, total.astype(jnp.bfloat16), preferred_element_type=jnp.float32)
        rank = (inside + ahead).astype(jnp.int32) - 1
        slot = slot + jnp.where(target == t, rank, 0)
    high = slot // LANES
    low = slot % LANES
    rows = slabs * cap // LANES
    for r in range(chunks):
        at = pl.ds(r * LANES, LANES)
        high_ref[:, at] = mask(iota((rows, LANES), 0) == high[r : r + 1, :])
        low_ref[:, at] = mask(iota((LANES, LANES), 0) == low[r : r + 1, :])
    codes = high_ref[...]
    for c in range(3):
        code_ref[c * rows : (c + 1) * rows, :] = codes * position_ref[c : c + 1, :].astype(jnp.bfloat16)
        code_ref[(3 + c) * rows : (4 + c) * rows, :] = codes * signs[8 + c : 9 + c, :].astype(jnp.bfloat16)
    slots = lax.dot_general(code_ref[...], low_ref[...], CONTRACT_LANES, preferred_element_type=jnp.float32)
    start_ref[...] = slots[: 3 * rows]
    course_ref[...] = slots[3 * rows :] * np.float32(1 / np.sqrt(2.0))
    fetch.wait()


def glide_kernel(order, slabs, *refs):
    pick_ref, mobility_ref, factor_ref, high_ref, low_ref, start_ref, course_ref, weight_ref = refs[:8]
    group = len(order)
    stress_refs = [refs[8 + order.index(k)] for k in range(group)]
    term_ref = refs[8 + group]
    keep_ref, send_ref = refs[9 + group : 11 + group]
    tiles_ref, step_ref, move_ref = refs[11 + group :]
    blocks = pick_ref.shape[0]
    held = stress_refs[0].shape[0] // NR
    for c in range(NR):
        stress = jnp.concatenate([ref[c * held : (c + 1) * held, :] for ref in stress_refs], axis=0)
        picked = jnp.dot(pick_ref[...], stress, preferred_element_type=jnp.float32)
        for j in range(0, blocks, SUB):
            tiles_ref[(j + c) * SUB : (j + c + 1) * SUB, :] = picked[j : j + SUB]

    span = PACK * SEGB
    part = iota((SUB, span), 1) // SEGB
    real = iota((SUB, span), 0) < NR
    for g in range(blocks // PACK):
        tiles = []
        for j in range(PACK):
            block = g * PACK + j
            tiles.append(tiles_ref[pl.ds(block // SUB * SUB * SUB + block % SUB, SUB, stride=SUB), :])
        stress = jnp.concatenate(tiles, axis=0).astype(jnp.bfloat16)
        at = pl.ds(g * span, span)
        crossed = lax.dot_general(stress, weight_ref[at, :], CONTRACT_LANES, preferred_element_type=jnp.float32)
        sampled = crossed[:SUB]
        for j in range(1, PACK):
            sampled = jnp.where(part == j, crossed[j * SUB : (j + 1) * SUB], sampled)
        factors = factor_ref[:, at]
        resolved = jnp.sum(jnp.where(real, factors * sampled, 0.0), axis=0, keepdims=True)
        step = glide_time * mobility_ref[:, at] * resolved
        step_ref[:, at] = step
        term_ref[:, at] = step * factors

    step = step_ref[...]
    high = high_ref[...]
    slot_rows = high.shape[0]
    deep = slot_rows // slabs
    step = lax.dot_general(high * step.astype(jnp.bfloat16), low_ref[...], CONTRACT_LANES, preferred_element_type=jnp.float32)
    for c in range(4):
        value = step
        if c < 3:
            at = slice(c * slot_rows, (c + 1) * slot_rows)
            value = start_ref[at, :] + course_ref[at, :] * step
        for t in range(slabs):
            row = (t * 4 + c) * deep
            move_ref[row : row + deep, :] = value[t * deep : (t + 1) * deep]
    half = keep_ref.shape[0]
    keep_ref[...] = move_ref[:half, :].astype(keep_ref.dtype)
    send_ref[...] = move_ref[half:, :].astype(send_ref.dtype)


def spread_kernel(group, *refs):
    put_ref, term_ref, weight_ref, kept_ref = refs[:4]
    sent_refs = refs[4 : 3 + group]
    spread_ref = refs[3 + group]
    blocks = put_ref.shape[1] // 2
    held = kept_ref.shape[0] // NR
    span = PACK * SEGB
    part = iota((SUB, span), 1) // SEGB
    for g in range(blocks // PACK):
        at = pl.ds(g * span, span)
        term = term_ref[:, at]
        term = jnp.concatenate([jnp.where(part == j, term, 0.0) for j in range(PACK)], axis=0).astype(jnp.bfloat16)
        spread_ref[g * PACK * SUB : (g + 1) * PACK * SUB, :] = jnp.dot(term, weight_ref[at, :], preferred_element_type=jnp.float32)
    for c in range(NR):
        spread = spread_ref[pl.ds(c, blocks, stride=SUB), :]
        rounded = spread.astype(jnp.bfloat16)
        rest = (spread - rounded.astype(jnp.float32)).astype(jnp.bfloat16)
        dense = jnp.dot(put_ref[...], jnp.concatenate([rounded, rest], axis=0), preferred_element_type=jnp.float32)
        rows = slice(c * held, (c + 1) * held)
        kept_ref[rows, :] = dense[:held]
        for k in range(1, group):
            sent_refs[k - 1][rows, :] = dense[k * held : (k + 1) * held].astype(jnp.bfloat16)


def gather_kernel(chunk, picks, *refs):
    for k, (which, place) in enumerate(picks):
        refs[-1][k * chunk : (k + 1) * chunk, :] = refs[which][place * chunk : (place + 1) * chunk, :]


def finish_kernel(group, slabs, picks, *refs):
    kept_ref = refs[0]
    got_refs = refs[1:group]
    moved_refs = refs[group:-4]
    distortion_ref, arrived_ref, sum_ref, slot_ref = refs[-4:]
    total = kept_ref[...]
    for ref in got_refs:
        total = total + ref[...].astype(jnp.float32)
    held = total.shape[0] // NR
    for c in range(NR):
        for b in range(0, held, SUB):
            sum_ref[b * NR + c * SUB : b * NR + (c + 1) * SUB, :] = total[c * held + b : c * held + b + SUB]
    for block in range(distortion_ref.shape[1] // LANES):
        part = sum_ref[pl.ds(block // SUB * NR * SUB + block % SUB, NR, stride=SUB), :]
        at = slice(block * LANES, (block + 1) * LANES)
        distortion_ref[:2, at] = part[:2]
        distortion_ref[2:3, at] = -(part[:1] + part[1:2])
        distortion_ref[3:, at] = part[2:]
    rows = slot_ref.shape[1]
    deep = rows // 4
    for source, (which, place) in picks.items():
        slot_ref[source] = moved_refs[which][place * rows : (place + 1) * rows, :].astype(jnp.float32)
    me = lax.axis_index("slab")
    for s in range(slabs):
        for b in range(deep):
            lane = (s * deep + b) * LANES
            arrived_ref[:, lane : lane + LANES] = slot_ref[me ^ s, pl.ds(b, 4, stride=deep), :]


def body(
    stress, interp_weight, block_owner, block_local, slip_system, mobility, position, target_slab
):
    group = lax.axis_size("grp")
    slabs = lax.axis_size("slab")
    segments = slip_system.shape[0]
    voxels = stress.shape[1]
    cap = 2 * segments // slabs
    slot_rows = slabs * cap // LANES
    f32, bf16 = jnp.float32, jnp.bfloat16
    shape = jax.ShapeDtypeStruct
    params = pltpu.CompilerParams(vmem_limit_bytes=48 * 1024 * 1024)

    def swap(x, k):
        return lax.ppermute(x, "grp", [(i, i ^ k) for i in range(group)])

    peers = sorted(range(1, group), key=lambda k: -bin(k).count("1"))
    blocks = block_local.shape[0]

    def still(x):
        return pltpu.with_memory_space_constraint(x, pltpu.HBM)

    packed, place = pl.pallas_call(
        pack_kernel,
        out_shape=(shape((NR * voxels // LANES, LANES), bf16), shape((1, blocks), jnp.int32)),
        in_specs=[HBM] * 3,
        out_specs=[VMEM] * 2,
        scratch_shapes=[
            pltpu.VMEM(stress.shape, bf16),
            pltpu.VMEM((NR * voxels // LANES, LANES), f32),
            pltpu.VMEM((2, 1, blocks), jnp.int32),
            pltpu.SemaphoreType.DMA((3,)),
        ],
        compiler_params=params,
        name="pack",
    )(still(stress), still(block_owner.reshape(1, blocks)), still(block_local.reshape(1, blocks)))
    parts = {k: swap(packed, k) for k in peers}
    parts[0] = packed
    order = [0, *peers]

    slot_shape = (3 * slot_rows, LANES)
    factor, high, low, pick, put, start, course, weight = pl.pallas_call(
        functools.partial(prepare_kernel, slabs, cap),
        out_shape=(
            shape((SUB, segments), f32),
            shape((slot_rows, segments), bf16),
            shape((LANES, segments), bf16),
            shape((blocks, group * voxels // BLK), bf16),
            shape((group * voxels // BLK, 2 * blocks), bf16),
            shape(slot_shape, f32),
            shape(slot_shape, f32),
            shape((segments, BLK), bf16),
        ),
        in_specs=[VMEM] * 4 + [HBM],
        out_specs=[VMEM] * 8,
        scratch_shapes=[pltpu.VMEM((6 * slot_rows, segments), bf16), pltpu.SemaphoreType.DMA],
        compiler_params=params,
        name="prepare",
    )(
        slip_system.reshape(1, segments),
        target_slab.reshape(segments // LANES, LANES),
        place,
        position,
        still(interp_weight.reshape(segments, BLK)),
    )

    chunk = 4 * slot_rows // slabs
    term, keep, send = pl.pallas_call(
        functools.partial(glide_kernel, order, slabs),
        out_shape=(shape((SUB, segments), f32),) + (shape((slabs // 2 * chunk, LANES), bf16),) * 2,
        in_specs=[VMEM] * (8 + group),
        out_specs=[VMEM] * 3,
        scratch_shapes=[
            pltpu.VMEM((SUB * blocks, LANES), f32),
            pltpu.VMEM((1, segments), f32),
            pltpu.VMEM((4 * slot_rows, LANES), f32),
        ],
        compiler_params=params,
        name="glide",
    )(
        pick,
        mobility.reshape(1, segments),
        factor,
        high,
        low,
        start,
        course,
        weight,
        *[parts[k] for k in order],
    )

    def hop(x, k):
        return lax.ppermute(x, "slab", [(i, i ^ k) for i in range(slabs)])

    bit = slabs // 2
    arrays = [keep, hop(send, bit)]
    held = {(r, s * bit): (s, r) for r in range(bit) for s in range(2)}
    while bit > 1:
        bit //= 2
        leaving = {key: at for key, at in sorted(held.items(), key=lambda item: item[0][::-1]) if key[0] & bit}
        send = pl.pallas_call(
            functools.partial(gather_kernel, chunk, tuple(leaving.values())),
            out_shape=shape((len(leaving) * chunk, LANES), bf16),
            in_specs=[VMEM] * len(arrays),
            out_specs=VMEM,
            compiler_params=params,
            name="gather",
        )(*arrays)
        for k, key in enumerate(leaving):
            del held[key]
            held[key[0] ^ bit, key[1] | bit] = (len(arrays), k)
        arrays.append(hop(send, bit))

    kept, *sent = pl.pallas_call(
        functools.partial(spread_kernel, group),
        out_shape=(shape(packed.shape, f32),) + (shape(packed.shape, bf16),) * (group - 1),
        in_specs=[VMEM] * 3,
        out_specs=[VMEM] * group,
        scratch_shapes=[pltpu.VMEM((blocks * SUB, LANES), f32)],
        compiler_params=params,
        name="spread",
    )(put, term, weight)
    got = [swap(sent[k - 1], k) for k in peers]
    return pl.pallas_call(
        functools.partial(finish_kernel, group, slabs, {s: at for (_, s), at in held.items()}),
        out_shape=(shape((NC, voxels), f32), shape((4, slabs * cap), f32)),
        in_specs=[VMEM] * (group + len(arrays)),
        out_specs=[VMEM] * 2,
        scratch_shapes=[
            pltpu.VMEM(packed.shape, f32),
            pltpu.VMEM((slabs, chunk, LANES), f32),
        ],
        compiler_params=params,
        name="finish",
    )(kept, *got, *arrays)


def solution(mesh):
    placed = (
        P(None, ("slab", "grp")),
        P(("slab", "grp"), None, None),
        P(("slab", "grp"), None),
        P(("slab", "grp")),
        P(("slab", "grp")),
        P(("slab", "grp")),
        P(None, ("slab", "grp")),
        P(("slab", "grp"), None),
    )
    return jax.shard_map(
        body,
        mesh=mesh,
        in_specs=placed,
        out_specs=(P(None, ("slab", "grp")), P(None, ("slab", "grp"))),
        check_vma=False,
    )
```

```python
import functools

import jax
import jax.numpy as jnp
import numpy as np
from jax import lax
from jax.experimental import pallas as pl
from jax.experimental.pallas import tpu as pltpu
from jax.sharding import PartitionSpec as P

NC = 6
NR = 5
NSYS = 12
BLK = 128
SEGB = 64
LANES = 128
SUB = 8
PACK = 8

glide_time = 0.5

VMEM = pl.BlockSpec(memory_space=pltpu.VMEM)
HBM = pl.BlockSpec(memory_space=pltpu.HBM)
CONTRACT_LANES = (((1,), (1,)), ((), ()))


def slip_signs():
    normal_list = [(1, 1, 1), (-1, 1, 1), (1, -1, 1), (1, 1, -1)]
    table = np.zeros((16, 16), np.int32)
    system = 0
    for x, y, z in normal_list:
        for burgers in ((y, -x, 0), (z, 0, -x), (0, z, -y)):
            outer = np.outer((x, y, z), burgers)
            tensor = outer + outer.T
            table[:NR, system] = (tensor[0, 0] // 2, tensor[1, 1] // 2, tensor[1, 2], tensor[0, 2], tensor[0, 1])
            table[8:11, system] = burgers
            system += 1
    return table


def iota(shape, dim):
    return lax.broadcasted_iota(jnp.int32, shape, dim)


def mask(condition):
    return jnp.where(condition, 1.0, 0.0).astype(jnp.bfloat16)


def pack_kernel(source_ref, owner_ref, local_ref, packed_ref, place_ref, stress_ref, rows_ref, block_ref, sems):
    copies = [
        pltpu.make_async_copy(source_ref, stress_ref, sems.at[0]),
        pltpu.make_async_copy(owner_ref, block_ref.at[0], sems.at[1]),
        pltpu.make_async_copy(local_ref, block_ref.at[1], sems.at[2]),
    ]
    for copy in copies:
        copy.start()
    for copy in copies:
        copy.wait()
    blocks = stress_ref.shape[1] // LANES
    place_ref[...] = (block_ref[0] ^ lax.axis_index("grp")) * blocks + block_ref[1]
    for block in range(blocks):
        stress = stress_ref[:, block * LANES : (block + 1) * LANES].astype(jnp.float32)
        row = block // SUB * NR * SUB + block % SUB
        rows_ref[pl.ds(row, 2, stride=SUB), :] = stress[:2] - stress[2:3]
        rows_ref[pl.ds(row + 2 * SUB, 3, stride=SUB), :] = stress[3:]
    for c in range(NR):
        pieces = [rows_ref[b * NR + c * SUB : b * NR + (c + 1) * SUB, :] for b in range(0, blocks, SUB)]
        packed_ref[c * blocks : (c + 1) * blocks, :] = jnp.concatenate(pieces, axis=0).astype(jnp.bfloat16)


def code_kernel(slabs, cap, target_ref, source_ref, high_ref, low_ref, weight_ref, sem):
    fetch = pltpu.make_async_copy(source_ref, weight_ref, sem)
    fetch.start()
    chunks = target_ref.shape[0]
    target = target_ref[...] ^ lax.axis_index("slab")
    upto = mask(iota((LANES, LANES), 0) <= iota((LANES, LANES), 1))
    ones = jnp.ones((LANES, LANES), jnp.bfloat16)
    before = mask(iota((chunks, chunks), 1) < iota((chunks, chunks), 0))
    slot = target * cap
    for t in range(slabs):
        here = mask(target == t)
        inside = jnp.dot(here, upto, preferred_element_type=jnp.float32)
        total = jnp.dot(here, ones, preferred_element_type=jnp.float32)
        ahead = jnp.dot(before, total.astype(jnp.bfloat16), preferred_element_type=jnp.float32)
        rank = (inside + ahead).astype(jnp.int32) - 1
        slot = slot + jnp.where(target == t, rank, 0)
    high = slot // LANES
    low = slot % LANES
    rows = slabs * cap // LANES
    for r in range(chunks):
        at = pl.ds(r * LANES, LANES)
        high_ref[:, at] = mask(iota((rows, LANES), 0) == high[r : r + 1, :])
        low_ref[:, at] = mask(iota((LANES, LANES), 0) == low[r : r + 1, :])
    fetch.wait()


def prepare_kernel(*refs):
    slip_ref, place_ref, position_ref, high_ref, low_ref = refs[:5]
    factor_ref, pick_ref, put_ref, start_ref, course_ref, code_ref = refs[5:]
    segments = slip_ref.shape[1]
    hot = mask(iota((16, segments), 0) == slip_ref[...])
    spot = iota((16, 16), 0) * 16 + iota((16, 16), 1)
    table = jnp.zeros((16, 16), jnp.float32)
    for (row, system), sign in np.ndenumerate(slip_signs()):
        if sign:
            table = jnp.where(spot == row * 16 + system, float(sign), table)
    signs = jnp.dot(table.astype(jnp.bfloat16), hot, preferred_element_type=jnp.float32)
    factor_ref[...] = signs[:SUB] * np.float32(1 / np.sqrt(6.0))
    blocks, choices = pick_ref.shape
    place = jnp.concatenate([place_ref[...], place_ref[...]], axis=1)
    put = jnp.where(iota((choices, 2 * blocks), 0) == place, 1.0, 0.0)
    put_ref[...] = put.astype(jnp.bfloat16)
    pick_ref[...] = put.T[:blocks].astype(jnp.bfloat16)
    codes = high_ref[...]
    rows = codes.shape[0]
    for c in range(3):
        code_ref[c * rows : (c + 1) * rows, :] = codes * position_ref[c : c + 1, :].astype(jnp.bfloat16)
        code_ref[(3 + c) * rows : (4 + c) * rows, :] = codes * signs[8 + c : 9 + c, :].astype(jnp.bfloat16)
    slots = lax.dot_general(code_ref[...], low_ref[...], CONTRACT_LANES, preferred_element_type=jnp.float32)
    start_ref[...] = slots[: 3 * rows]
    course_ref[...] = slots[3 * rows :] * np.float32(1 / np.sqrt(2.0))


def glide_kernel(order, slabs, *refs):
    pick_ref, mobility_ref, factor_ref, high_ref, low_ref, start_ref, course_ref, weight_ref = refs[:8]
    group = len(order)
    stress_refs = [refs[8 + order.index(k)] for k in range(group)]
    term_ref = refs[8 + group]
    keep_ref, send_ref = refs[9 + group : 11 + group]
    step_ref, move_ref = refs[11 + group :]
    blocks = pick_ref.shape[0]
    held = stress_refs[0].shape[0] // NR
    picked = []
    for c in range(NR):
        stress = jnp.concatenate([ref[c * held : (c + 1) * held, :] for ref in stress_refs], axis=0)
        picked.append(jnp.dot(pick_ref[...], stress, preferred_element_type=jnp.float32))

    span = PACK * SEGB
    mine = iota((PACK, span), 0) == iota((PACK, span), 1) // SEGB
    for g in range(blocks // PACK):
        stress = jnp.concatenate([x[g * PACK : (g + 1) * PACK] for x in picked], axis=0).astype(jnp.bfloat16)
        at = pl.ds(g * span, span)
        sampled = lax.dot_general(stress, weight_ref[at, :], CONTRACT_LANES, preferred_element_type=jnp.float32)
        resolved = sampled[:PACK] * factor_ref[:1, at]
        for c in range(1, NR):
            resolved = resolved + sampled[c * PACK : (c + 1) * PACK] * factor_ref[c : c + 1, at]
        resolved = jnp.sum(jnp.where(mine, resolved, 0.0), axis=0, keepdims=True)
        step = glide_time * mobility_ref[:, at] * resolved
        step_ref[:, at] = step
        term_ref[:, at] = step * factor_ref[:, at]

    step = step_ref[...]
    high = high_ref[...]
    slot_rows = high.shape[0]
    deep = slot_rows // slabs
    step = lax.dot_general(high * step.astype(jnp.bfloat16), low_ref[...], CONTRACT_LANES, preferred_element_type=jnp.float32)
    for c in range(4):
        value = step
        if c < 3:
            at = slice(c * slot_rows, (c + 1) * slot_rows)
            value = start_ref[at, :] + course_ref[at, :] * step
        for t in range(slabs):
            row = (t * 4 + c) * deep
            move_ref[row : row + deep, :] = value[t * deep : (t + 1) * deep]
    half = keep_ref.shape[0]
    keep_ref[...] = move_ref[:half, :].astype(keep_ref.dtype)
    send_ref[...] = move_ref[half:, :].astype(send_ref.dtype)


def spread_kernel(group, *refs):
    put_ref, term_ref, weight_ref, kept_ref = refs[:4]
    sent_refs = refs[4 : 3 + group]
    blocks = put_ref.shape[1] // 2
    held = kept_ref.shape[0] // NR
    span = PACK * SEGB
    mine = iota((PACK, span), 0) == iota((PACK, span), 1) // SEGB
    parts = []
    for g in range(blocks // PACK):
        at = pl.ds(g * span, span)
        terms = [jnp.where(mine, term_ref[c : c + 1, at], 0.0) for c in range(NR)]
        terms = jnp.concatenate(terms, axis=0).astype(jnp.bfloat16)
        parts.append(jnp.dot(terms, weight_ref[at, :], preferred_element_type=jnp.float32))
    for c in range(NR):
        spread = jnp.concatenate([x[c * PACK : (c + 1) * PACK] for x in parts], axis=0)
        rounded = spread.astype(jnp.bfloat16)
        rest = (spread - rounded.astype(jnp.float32)).astype(jnp.bfloat16)
        dense = jnp.dot(put_ref[...], jnp.concatenate([rounded, rest], axis=0), preferred_element_type=jnp.float32)
        rows = slice(c * held, (c + 1) * held)
        kept_ref[rows, :] = dense[:held]
        for k in range(1, group):
            sent_refs[k - 1][rows, :] = dense[k * held : (k + 1) * held].astype(jnp.bfloat16)


def gather_kernel(chunk, picks, *refs):
    for k, (which, place) in enumerate(picks):
        refs[-1][k * chunk : (k + 1) * chunk, :] = refs[which][place * chunk : (place + 1) * chunk, :]


def total_kernel(*refs):
    kept_ref, got_refs = refs[0], refs[1:-2]
    distortion_ref, sum_ref = refs[-2:]
    total = kept_ref[...]
    for ref in got_refs:
        total = total + ref[...].astype(jnp.float32)
    held = total.shape[0] // NR
    for c in range(NR):
        for b in range(0, held, SUB):
            sum_ref[b * NR + c * SUB : b * NR + (c + 1) * SUB, :] = total[c * held + b : c * held + b + SUB]
    for block in range(held):
        part = sum_ref[pl.ds(block // SUB * NR * SUB + block % SUB, NR, stride=SUB), :]
        at = slice(block * LANES, (block + 1) * LANES)
        distortion_ref[:2, at] = part[:2]
        distortion_ref[2:3, at] = -(part[:1] + part[1:2])
        distortion_ref[3:, at] = part[2:]


def arrive_kernel(slabs, picks, *refs):
    moved_refs = refs[:-2]
    arrived_ref, slot_ref = refs[-2:]
    rows = slot_ref.shape[1]
    deep = rows // 4
    for source, (which, place) in picks.items():
        slot_ref[source] = moved_refs[which][place * rows : (place + 1) * rows, :].astype(jnp.float32)
    me = lax.axis_index("slab")
    for s in range(slabs):
        for b in range(deep):
            lane = (s * deep + b) * LANES
            arrived_ref[:, lane : lane + LANES] = slot_ref[me ^ s, pl.ds(b, 4, stride=deep), :]


def body(
    stress, interp_weight, block_owner, block_local, slip_system, mobility, position, target_slab
):
    group = lax.axis_size("grp")
    slabs = lax.axis_size("slab")
    segments = slip_system.shape[0]
    voxels = stress.shape[1]
    cap = 2 * segments // slabs
    slot_rows = slabs * cap // LANES
    f32, bf16 = jnp.float32, jnp.bfloat16
    shape = jax.ShapeDtypeStruct
    params = pltpu.CompilerParams(vmem_limit_bytes=48 * 1024 * 1024)

    def swap(x, k):
        return lax.ppermute(x, "grp", [(i, i ^ k) for i in range(group)])

    peers = sorted(range(1, group), key=lambda k: -bin(k).count("1"))
    blocks = block_local.shape[0]

    def still(x):
        return pltpu.with_memory_space_constraint(x, pltpu.HBM)

    packed, place = pl.pallas_call(
        pack_kernel,
        out_shape=(shape((NR * voxels // LANES, LANES), bf16), shape((1, blocks), jnp.int32)),
        in_specs=[HBM] * 3,
        out_specs=[VMEM] * 2,
        scratch_shapes=[
            pltpu.VMEM(stress.shape, bf16),
            pltpu.VMEM((NR * voxels // LANES, LANES), f32),
            pltpu.VMEM((2, 1, blocks), jnp.int32),
            pltpu.SemaphoreType.DMA((3,)),
        ],
        compiler_params=params,
        name="pack",
    )(still(stress), still(block_owner.reshape(1, blocks)), still(block_local.reshape(1, blocks)))
    parts = {k: swap(packed, k) for k in peers}
    parts[0] = packed
    order = [0, *peers]

    slot_shape = (3 * slot_rows, LANES)
    high, low, weight = pl.pallas_call(
        functools.partial(code_kernel, slabs, cap),
        out_shape=(
            shape((slot_rows, segments), bf16),
            shape((LANES, segments), bf16),
            shape((segments, BLK), bf16),
        ),
        in_specs=[VMEM, HBM],
        out_specs=[VMEM] * 3,
        scratch_shapes=[pltpu.SemaphoreType.DMA],
        compiler_params=params,
        name="code",
    )(target_slab.reshape(segments // LANES, LANES), still(interp_weight.reshape(segments, BLK)))
    factor, pick, put, start, course = pl.pallas_call(
        prepare_kernel,
        out_shape=(
            shape((SUB, segments), f32),
            shape((blocks, group * voxels // BLK), bf16),
            shape((group * voxels // BLK, 2 * blocks), bf16),
            shape(slot_shape, f32),
            shape(slot_shape, f32),
        ),
        in_specs=[VMEM] * 5,
        out_specs=[VMEM] * 5,
        scratch_shapes=[pltpu.VMEM((6 * slot_rows, segments), bf16)],
        compiler_params=params,
        name="prepare",
    )(slip_system.reshape(1, segments), place, position, high, low)

    chunk = 4 * slot_rows // slabs
    term, keep, send = pl.pallas_call(
        functools.partial(glide_kernel, order, slabs),
        out_shape=(shape((SUB, segments), f32),) + (shape((slabs // 2 * chunk, LANES), bf16),) * 2,
        in_specs=[VMEM] * (8 + group),
        out_specs=[VMEM] * 3,
        scratch_shapes=[
            pltpu.VMEM((1, segments), f32),
            pltpu.VMEM((4 * slot_rows, LANES), f32),
        ],
        compiler_params=params,
        name="glide",
    )(
        pick,
        mobility.reshape(1, segments),
        factor,
        high,
        low,
        start,
        course,
        weight,
        *[parts[k] for k in order],
    )

    def hop(x, k):
        return lax.ppermute(x, "slab", [(i, i ^ k) for i in range(slabs)])

    bit = slabs // 2
    arrays = [keep, hop(send, bit)]
    held = {(r, s * bit): (s, r) for r in range(bit) for s in range(2)}
    while bit > 1:
        bit //= 2
        leaving = {key: at for key, at in sorted(held.items(), key=lambda item: item[0][::-1]) if key[0] & bit}
        send = pl.pallas_call(
            functools.partial(gather_kernel, chunk, tuple(leaving.values())),
            out_shape=shape((len(leaving) * chunk, LANES), bf16),
            in_specs=[VMEM] * len(arrays),
            out_specs=VMEM,
            compiler_params=params,
            name="gather",
        )(*arrays)
        for k, key in enumerate(leaving):
            del held[key]
            held[key[0] ^ bit, key[1] | bit] = (len(arrays), k)
        arrays.append(hop(send, bit))

    kept, *sent = pl.pallas_call(
        functools.partial(spread_kernel, group),
        out_shape=(shape(packed.shape, f32),) + (shape(packed.shape, bf16),) * (group - 1),
        in_specs=[VMEM] * 3,
        out_specs=[VMEM] * group,
        compiler_params=params,
        name="spread",
    )(put, term, weight)
    got = [swap(sent[k - 1], k) for k in peers]
    distortion = pl.pallas_call(
        total_kernel,
        out_shape=shape((NC, voxels), f32),
        in_specs=[VMEM] * group,
        out_specs=VMEM,
        scratch_shapes=[pltpu.VMEM(packed.shape, f32)],
        compiler_params=params,
        name="total",
    )(kept, *got)
    arrived = pl.pallas_call(
        functools.partial(arrive_kernel, slabs, {s: at for (_, s), at in held.items()}),
        out_shape=shape((4, slabs * cap), f32),
        in_specs=[VMEM] * len(arrays),
        out_specs=VMEM,
        scratch_shapes=[pltpu.VMEM((slabs, chunk, LANES), f32)],
        compiler_params=params,
        name="arrive",
    )(*arrays)
    return (distortion, arrived)


def solution(mesh):
    placed = (
        P(None, ("slab", "grp")),
        P(("slab", "grp"), None, None),
        P(("slab", "grp"), None),
        P(("slab", "grp")),
        P(("slab", "grp")),
        P(("slab", "grp")),
        P(None, ("slab", "grp")),
        P(("slab", "grp"), None),
    )
    return jax.shard_map(
        body,
        mesh=mesh,
        in_specs=placed,
        out_specs=(P(None, ("slab", "grp")), P(None, ("slab", "grp"))),
        check_vma=False,
    )
```

```python
import functools

import jax
import jax.numpy as jnp
import numpy as np
from jax import lax
from jax.experimental import pallas as pl
from jax.experimental.pallas import tpu as pltpu
from jax.sharding import PartitionSpec as P

NC = 6
NR = 5
NSYS = 12
BLK = 128
SEGB = 64
LANES = 128
SUB = 8
PACK = 8

glide_time = 0.5

VMEM = pl.BlockSpec(memory_space=pltpu.VMEM)
HBM = pl.BlockSpec(memory_space=pltpu.HBM)
CONTRACT_LANES = (((1,), (1,)), ((), ()))


def slip_signs():
    normal_list = [(1, 1, 1), (-1, 1, 1), (1, -1, 1), (1, 1, -1)]
    table = np.zeros((16, 16), np.int32)
    system = 0
    for x, y, z in normal_list:
        for burgers in ((y, -x, 0), (z, 0, -x), (0, z, -y)):
            outer = np.outer((x, y, z), burgers)
            tensor = outer + outer.T
            table[:NR, system] = (tensor[0, 0] // 2, tensor[1, 1] // 2, tensor[1, 2], tensor[0, 2], tensor[0, 1])
            table[8:11, system] = burgers
            system += 1
    return table


def iota(shape, dim):
    return lax.broadcasted_iota(jnp.int32, shape, dim)


def mask(condition):
    return jnp.where(condition, 1.0, 0.0).astype(jnp.bfloat16)


def turned(index, group):
    side = group.bit_length() // 2
    return (index & ((1 << side) - 1)) << side | index >> side


def pack_kernel(group, source_ref, owner_ref, local_ref, packed_ref, place_ref, stress_ref, rows_ref, block_ref, sems):
    copies = [
        pltpu.make_async_copy(source_ref, stress_ref, sems.at[0]),
        pltpu.make_async_copy(owner_ref, block_ref.at[0], sems.at[1]),
        pltpu.make_async_copy(local_ref, block_ref.at[1], sems.at[2]),
    ]
    for copy in copies:
        copy.start()
    for copy in copies:
        copy.wait()
    blocks = stress_ref.shape[1] // LANES
    across = block_ref[0] ^ lax.axis_index("grp")
    across = jnp.where(lax.axis_index("slab") % 2 == 1, turned(across, group), across)
    place_ref[...] = across * blocks + block_ref[1]
    for block in range(blocks):
        stress = stress_ref[:, block * LANES : (block + 1) * LANES].astype(jnp.float32)
        row = block // SUB * NR * SUB + block % SUB
        rows_ref[pl.ds(row, 2, stride=SUB), :] = stress[:2] - stress[2:3]
        rows_ref[pl.ds(row + 2 * SUB, 3, stride=SUB), :] = stress[3:]
    for c in range(NR):
        pieces = [rows_ref[b * NR + c * SUB : b * NR + (c + 1) * SUB, :] for b in range(0, blocks, SUB)]
        packed_ref[c * blocks : (c + 1) * blocks, :] = jnp.concatenate(pieces, axis=0).astype(jnp.bfloat16)


def code_kernel(slabs, cap, target_ref, source_ref, high_ref, low_ref, weight_ref, sem):
    fetch = pltpu.make_async_copy(source_ref, weight_ref, sem)
    fetch.start()
    chunks = target_ref.shape[0]
    target = target_ref[...] ^ lax.axis_index("slab")
    upto = mask(iota((LANES, LANES), 0) <= iota((LANES, LANES), 1))
    ones = jnp.ones((LANES, LANES), jnp.bfloat16)
    before = mask(iota((chunks, chunks), 1) < iota((chunks, chunks), 0))
    slot = target * cap
    for t in range(slabs):
        here = mask(target == t)
        inside = jnp.dot(here, upto, preferred_element_type=jnp.float32)
        total = jnp.dot(here, ones, preferred_element_type=jnp.float32)
        ahead = jnp.dot(before, total.astype(jnp.bfloat16), preferred_element_type=jnp.float32)
        rank = (inside + ahead).astype(jnp.int32) - 1
        slot = slot + jnp.where(target == t, rank, 0)
    high = slot // LANES
    low = slot % LANES
    rows = slabs * cap // LANES
    for r in range(chunks):
        at = pl.ds(r * LANES, LANES)
        high_ref[:, at] = mask(iota((rows, LANES), 0) == high[r : r + 1, :])
        low_ref[:, at] = mask(iota((LANES, LANES), 0) == low[r : r + 1, :])
    fetch.wait()


def prepare_kernel(*refs):
    slip_ref, place_ref, position_ref, high_ref, low_ref = refs[:5]
    factor_ref, pick_ref, put_ref, start_ref, course_ref, code_ref = refs[5:]
    segments = slip_ref.shape[1]
    hot = mask(iota((16, segments), 0) == slip_ref[...])
    spot = iota((16, 16), 0) * 16 + iota((16, 16), 1)
    table = jnp.zeros((16, 16), jnp.float32)
    for (row, system), sign in np.ndenumerate(slip_signs()):
        if sign:
            table = jnp.where(spot == row * 16 + system, float(sign), table)
    signs = jnp.dot(table.astype(jnp.bfloat16), hot, preferred_element_type=jnp.float32)
    factor_ref[...] = signs[:SUB] * np.float32(1 / np.sqrt(6.0))
    blocks, choices = pick_ref.shape
    place = jnp.concatenate([place_ref[...], place_ref[...]], axis=1)
    put = jnp.where(iota((choices, 2 * blocks), 0) == place, 1.0, 0.0)
    put_ref[...] = put.astype(jnp.bfloat16)
    pick_ref[...] = put.T[:blocks].astype(jnp.bfloat16)
    codes = high_ref[...]
    rows = codes.shape[0]
    for c in range(3):
        code_ref[c * rows : (c + 1) * rows, :] = codes * position_ref[c : c + 1, :].astype(jnp.bfloat16)
        code_ref[(3 + c) * rows : (4 + c) * rows, :] = codes * signs[8 + c : 9 + c, :].astype(jnp.bfloat16)
    slots = lax.dot_general(code_ref[...], low_ref[...], CONTRACT_LANES, preferred_element_type=jnp.float32)
    start_ref[...] = slots[: 3 * rows]
    course_ref[...] = slots[3 * rows :] * np.float32(1 / np.sqrt(2.0))


def glide_kernel(order, slabs, *refs):
    pick_ref, mobility_ref, factor_ref, high_ref, low_ref, start_ref, course_ref, weight_ref = refs[:8]
    group = len(order)
    stress_refs = [refs[8 + order.index(k)] for k in range(group)]
    term_ref = refs[8 + group]
    keep_ref, send_ref = refs[9 + group : 11 + group]
    step_ref, move_ref = refs[11 + group :]
    blocks = pick_ref.shape[0]
    held = stress_refs[0].shape[0] // NR
    picked = []
    for c in range(NR):
        stress = jnp.concatenate([ref[c * held : (c + 1) * held, :] for ref in stress_refs], axis=0)
        picked.append(jnp.dot(pick_ref[...], stress, preferred_element_type=jnp.float32))

    span = PACK * SEGB
    mine = iota((PACK, span), 0) == iota((PACK, span), 1) // SEGB
    for g in range(blocks // PACK):
        stress = jnp.concatenate([x[g * PACK : (g + 1) * PACK] for x in picked], axis=0).astype(jnp.bfloat16)
        at = pl.ds(g * span, span)
        sampled = lax.dot_general(stress, weight_ref[at, :], CONTRACT_LANES, preferred_element_type=jnp.float32)
        resolved = sampled[:PACK] * factor_ref[:1, at]
        for c in range(1, NR):
            resolved = resolved + sampled[c * PACK : (c + 1) * PACK] * factor_ref[c : c + 1, at]
        resolved = jnp.sum(jnp.where(mine, resolved, 0.0), axis=0, keepdims=True)
        step = glide_time * mobility_ref[:, at] * resolved
        step_ref[:, at] = step
        term_ref[:, at] = step * factor_ref[:, at]

    step = step_ref[...]
    high = high_ref[...]
    slot_rows = high.shape[0]
    deep = slot_rows // slabs
    step = lax.dot_general(high * step.astype(jnp.bfloat16), low_ref[...], CONTRACT_LANES, preferred_element_type=jnp.float32)
    for c in range(4):
        value = step
        if c < 3:
            at = slice(c * slot_rows, (c + 1) * slot_rows)
            value = start_ref[at, :] + course_ref[at, :] * step
        for t in range(slabs):
            row = ((t % 2 * slabs + t) // 2 * 4 + c) * deep
            move_ref[row : row + deep, :] = value[t * deep : (t + 1) * deep]
    half = keep_ref.shape[0]
    keep_ref[...] = move_ref[:half, :].astype(keep_ref.dtype)
    send_ref[...] = move_ref[half:, :].astype(send_ref.dtype)


def spread_kernel(group, *refs):
    put_ref, term_ref, weight_ref, kept_ref = refs[:4]
    sent_refs = refs[4 : 3 + group]
    blocks = put_ref.shape[1] // 2
    held = kept_ref.shape[0] // NR
    span = PACK * SEGB
    mine = iota((PACK, span), 0) == iota((PACK, span), 1) // SEGB
    parts = []
    for g in range(blocks // PACK):
        at = pl.ds(g * span, span)
        terms = [jnp.where(mine, term_ref[c : c + 1, at], 0.0) for c in range(NR)]
        terms = jnp.concatenate(terms, axis=0).astype(jnp.bfloat16)
        parts.append(jnp.dot(terms, weight_ref[at, :], preferred_element_type=jnp.float32))
    for c in range(NR):
        spread = jnp.concatenate([x[c * PACK : (c + 1) * PACK] for x in parts], axis=0)
        rounded = spread.astype(jnp.bfloat16)
        rest = (spread - rounded.astype(jnp.float32)).astype(jnp.bfloat16)
        dense = jnp.dot(put_ref[...], jnp.concatenate([rounded, rest], axis=0), preferred_element_type=jnp.float32)
        rows = slice(c * held, (c + 1) * held)
        kept_ref[rows, :] = dense[:held]
        for k in range(1, group):
            sent_refs[k - 1][rows, :] = dense[k * held : (k + 1) * held].astype(jnp.bfloat16)


def gather_kernel(chunk, picks, *refs):
    for k, (which, place) in enumerate(picks):
        refs[-1][k * chunk : (k + 1) * chunk, :] = refs[which][place * chunk : (place + 1) * chunk, :]
    rest = len(picks) * chunk
    refs[-1][rest:, :] = jnp.zeros((refs[-1].shape[0] - rest, LANES), refs[-1].dtype)


def total_kernel(*refs):
    kept_ref, got_refs = refs[0], refs[1:-2]
    distortion_ref, sum_ref = refs[-2:]
    total = kept_ref[...]
    for ref in got_refs:
        total = total + ref[...].astype(jnp.float32)
    held = total.shape[0] // NR
    for c in range(NR):
        for b in range(0, held, SUB):
            sum_ref[b * NR + c * SUB : b * NR + (c + 1) * SUB, :] = total[c * held + b : c * held + b + SUB]
    for block in range(held):
        part = sum_ref[pl.ds(block // SUB * NR * SUB + block % SUB, NR, stride=SUB), :]
        at = slice(block * LANES, (block + 1) * LANES)
        distortion_ref[:2, at] = part[:2]
        distortion_ref[2:3, at] = -(part[:1] + part[1:2])
        distortion_ref[3:, at] = part[2:]


def arrive_kernel(slabs, picks, *refs):
    moved_refs = refs[:-2]
    arrived_ref, slot_ref = refs[-2:]
    rows = slot_ref.shape[1]
    deep = rows // 4
    for source, (which, place) in picks.items():
        slot_ref[source] = moved_refs[which][place * rows : (place + 1) * rows, :].astype(jnp.float32)
    me = lax.axis_index("slab")
    for s in range(slabs):
        for b in range(deep):
            lane = (s * deep + b) * LANES
            arrived_ref[:, lane : lane + LANES] = slot_ref[me ^ s, pl.ds(b, 4, stride=deep), :]


def body(
    stress, interp_weight, block_owner, block_local, slip_system, mobility, position, target_slab
):
    group = lax.axis_size("grp")
    slabs = lax.axis_size("slab")
    segments = slip_system.shape[0]
    voxels = stress.shape[1]
    cap = 2 * segments // slabs
    slot_rows = slabs * cap // LANES
    f32, bf16 = jnp.float32, jnp.bfloat16
    shape = jax.ShapeDtypeStruct
    params = pltpu.CompilerParams(vmem_limit_bytes=48 * 1024 * 1024)

    def swap(x, k):
        steps = (k, turned(k, group))
        pairs = [(s * group + g, s * group + (g ^ steps[s % 2])) for s in range(slabs) for g in range(group)]
        return lax.ppermute(x, ("slab", "grp"), pairs)

    peers = sorted(range(1, group), key=lambda k: -bin(k).count("1"))
    blocks = block_local.shape[0]

    def still(x):
        return pltpu.with_memory_space_constraint(x, pltpu.HBM)

    packed, place = pl.pallas_call(
        functools.partial(pack_kernel, group),
        out_shape=(shape((NR * voxels // LANES, LANES), bf16), shape((1, blocks), jnp.int32)),
        in_specs=[HBM] * 3,
        out_specs=[VMEM] * 2,
        scratch_shapes=[
            pltpu.VMEM(stress.shape, bf16),
            pltpu.VMEM((NR * voxels // LANES, LANES), f32),
            pltpu.VMEM((2, 1, blocks), jnp.int32),
            pltpu.SemaphoreType.DMA((3,)),
        ],
        compiler_params=params,
        name="pack",
    )(still(stress), still(block_owner.reshape(1, blocks)), still(block_local.reshape(1, blocks)))
    parts = {k: swap(packed, k) for k in peers}
    parts[0] = packed
    order = [0, *peers]

    slot_shape = (3 * slot_rows, LANES)
    high, low, weight = pl.pallas_call(
        functools.partial(code_kernel, slabs, cap),
        out_shape=(
            shape((slot_rows, segments), bf16),
            shape((LANES, segments), bf16),
            shape((segments, BLK), bf16),
        ),
        in_specs=[VMEM, HBM],
        out_specs=[VMEM] * 3,
        scratch_shapes=[pltpu.SemaphoreType.DMA],
        compiler_params=params,
        name="code",
    )(target_slab.reshape(segments // LANES, LANES), still(interp_weight.reshape(segments, BLK)))
    factor, pick, put, start, course = pl.pallas_call(
        prepare_kernel,
        out_shape=(
            shape((SUB, segments), f32),
            shape((blocks, group * voxels // BLK), bf16),
            shape((group * voxels // BLK, 2 * blocks), bf16),
            shape(slot_shape, f32),
            shape(slot_shape, f32),
        ),
        in_specs=[VMEM] * 5,
        out_specs=[VMEM] * 5,
        scratch_shapes=[pltpu.VMEM((6 * slot_rows, segments), bf16)],
        compiler_params=params,
        name="prepare",
    )(slip_system.reshape(1, segments), place, position, high, low)

    chunk = 4 * slot_rows // slabs
    term, keep, send = pl.pallas_call(
        functools.partial(glide_kernel, order, slabs),
        out_shape=(shape((SUB, segments), f32),) + (shape((slabs // 2 * chunk, LANES), bf16),) * 2,
        in_specs=[VMEM] * (8 + group),
        out_specs=[VMEM] * 3,
        scratch_shapes=[
            pltpu.VMEM((1, segments), f32),
            pltpu.VMEM((4 * slot_rows, LANES), f32),
        ],
        compiler_params=params,
        name="glide",
    )(
        pick,
        mobility.reshape(1, segments),
        factor,
        high,
        low,
        start,
        course,
        weight,
        *[parts[k] for k in order],
    )

    def hop(x, k):
        return lax.ppermute(x, "slab", [(i, i ^ k) for i in range(slabs)])

    arrays = [keep, hop(send, 1)]
    held = {(r, s): (s, r // 2) for r in range(0, slabs, 2) for s in range(2)}
    kept, *sent = pl.pallas_call(
        functools.partial(spread_kernel, group),
        out_shape=(shape(packed.shape, f32),) + (shape(packed.shape, bf16),) * (group - 1),
        in_specs=[VMEM] * 3,
        out_specs=[VMEM] * group,
        compiler_params=params,
        name="spread",
    )(put, term, weight)
    bit = slabs
    while bit > 2:
        bit //= 2
        leaving = {key: at for key, at in sorted(held.items(), key=lambda item: item[0][::-1]) if key[0] & bit}
        through = tuple(sent) if bit == slabs // 2 else ()
        *through, send = pl.pallas_call(
            functools.partial(gather_kernel, chunk, tuple(leaving.values())),
            out_shape=tuple(shape(x.shape, x.dtype) for x in through) + (shape((len(leaving) * chunk + 48, LANES), bf16),),
            in_specs=[VMEM] * (len(arrays) + len(through)),
            out_specs=[VMEM] * (len(through) + 1),
            input_output_aliases={len(arrays) + k: k for k in range(len(through))},
            compiler_params=params,
            name="gather",
        )(*arrays, *through)
        sent = through or sent
        for k, key in enumerate(leaving):
            del held[key]
            held[key[0] ^ bit, key[1] | bit] = (len(arrays), k)
        arrays.append(hop(send, bit))
    got = [swap(sent[k - 1], k) for k in peers]

    distortion = pl.pallas_call(
        total_kernel,
        out_shape=shape((NC, voxels), f32),
        in_specs=[VMEM] * group,
        out_specs=VMEM,
        scratch_shapes=[pltpu.VMEM(packed.shape, f32)],
        compiler_params=params,
        name="total",
    )(kept, *got)
    arrived = pl.pallas_call(
        functools.partial(arrive_kernel, slabs, {s: at for (_, s), at in held.items()}),
        out_shape=shape((4, slabs * cap), f32),
        in_specs=[VMEM] * len(arrays),
        out_specs=VMEM,
        scratch_shapes=[pltpu.VMEM((slabs, chunk, LANES), f32)],
        compiler_params=params,
        name="arrive",
    )(*arrays)
    return (distortion, arrived)


def solution(mesh):
    placed = (
        P(None, ("slab", "grp")),
        P(("slab", "grp"), None, None),
        P(("slab", "grp"), None),
        P(("slab", "grp")),
        P(("slab", "grp")),
        P(("slab", "grp")),
        P(None, ("slab", "grp")),
        P(("slab", "grp"), None),
    )
    return jax.shard_map(
        body,
        mesh=mesh,
        in_specs=placed,
        out_specs=(P(None, ("slab", "grp")), P(None, ("slab", "grp"))),
        check_vma=False,
    )
```

```python
import functools

import jax
import jax.numpy as jnp
import numpy as np
from jax import lax
from jax.experimental import pallas as pl
from jax.experimental.pallas import tpu as pltpu
from jax.sharding import PartitionSpec as P

NC = 6
NR = 5
NSYS = 12
BLK = 128
SEGB = 64
LANES = 128
SUB = 8
PACK = 8

glide_time = 0.5

VMEM = pl.BlockSpec(memory_space=pltpu.VMEM)
HBM = pl.BlockSpec(memory_space=pltpu.HBM)
CONTRACT_LANES = (((1,), (1,)), ((), ()))


def slip_signs():
    normal_list = [(1, 1, 1), (-1, 1, 1), (1, -1, 1), (1, 1, -1)]
    table = np.zeros((16, 16), np.int32)
    system = 0
    for x, y, z in normal_list:
        for burgers in ((y, -x, 0), (z, 0, -x), (0, z, -y)):
            outer = np.outer((x, y, z), burgers)
            tensor = outer + outer.T
            table[:NR, system] = (tensor[0, 0] // 2, tensor[1, 1] // 2, tensor[1, 2], tensor[0, 2], tensor[0, 1])
            table[8:11, system] = burgers
            system += 1
    return table


def iota(shape, dim):
    return lax.broadcasted_iota(jnp.int32, shape, dim)


def mask(condition):
    return jnp.where(condition, 1.0, 0.0).astype(jnp.bfloat16)


def turned(index, group):
    side = group.bit_length() // 2
    return (index & ((1 << side) - 1)) << side | index >> side


def pack_kernel(group, source_ref, owner_ref, local_ref, packed_ref, place_ref, stress_ref, rows_ref, block_ref, sems):
    copies = [
        pltpu.make_async_copy(source_ref, stress_ref, sems.at[0]),
        pltpu.make_async_copy(owner_ref, block_ref.at[0], sems.at[1]),
        pltpu.make_async_copy(local_ref, block_ref.at[1], sems.at[2]),
    ]
    for copy in copies:
        copy.start()
    for copy in copies:
        copy.wait()
    blocks = stress_ref.shape[1] // LANES
    across = block_ref[0] ^ lax.axis_index("grp")
    across = jnp.where(lax.axis_index("slab") % 2 == 1, turned(across, group), across)
    place_ref[...] = across * blocks + block_ref[1]
    for block in range(blocks):
        at = pl.ds(block // SUB * NC * SUB + block % SUB, NC, stride=SUB)
        rows_ref[at, :] = stress_ref[:, block * LANES : (block + 1) * LANES].astype(jnp.float32)

    def component(c):
        pieces = [rows_ref[b * NC + c * SUB : b * NC + (c + 1) * SUB, :] for b in range(0, blocks, SUB)]
        return jnp.concatenate(pieces, axis=0)

    xx, yy, zz, yz, xz, xy = [component(c) for c in range(NC)]
    for c, value in enumerate((xx - zz, yy - zz, yz, xz, xy)):
        packed_ref[c * blocks : (c + 1) * blocks, :] = value.astype(jnp.bfloat16)


def code_kernel(slabs, cap, target_ref, source_ref, high_ref, low_ref, weight_ref, sem):
    fetch = pltpu.make_async_copy(source_ref, weight_ref, sem)
    fetch.start()
    chunks = target_ref.shape[0]
    target = target_ref[...] ^ lax.axis_index("slab")
    upto = mask(iota((LANES, LANES), 0) <= iota((LANES, LANES), 1))
    ones = jnp.ones((LANES, LANES), jnp.bfloat16)
    before = mask(iota((chunks, chunks), 1) < iota((chunks, chunks), 0))
    slot = target * cap
    for t in range(slabs):
        here = mask(target == t)
        inside = jnp.dot(here, upto, preferred_element_type=jnp.float32)
        total = jnp.dot(here, ones, preferred_element_type=jnp.float32)
        ahead = jnp.dot(before, total.astype(jnp.bfloat16), preferred_element_type=jnp.float32)
        rank = (inside + ahead).astype(jnp.int32) - 1
        slot = slot + jnp.where(target == t, rank, 0)
    high = slot // LANES
    low = (slot % LANES).T
    rows = slabs * cap // LANES
    for r in range(chunks):
        at = pl.ds(r * LANES, LANES)
        high_ref[:, at] = mask(iota((rows, LANES), 0) == high[r : r + 1, :])
        low_ref[at, :] = mask(iota((LANES, LANES), 1) == low[:, r : r + 1])
    fetch.wait()


def prepare_kernel(*refs):
    slip_ref, place_ref, position_ref, high_ref, low_ref = refs[:5]
    factor_ref, pick_ref, put_ref, start_ref, course_ref, code_ref = refs[5:]
    segments = slip_ref.shape[1]
    hot = mask(iota((16, segments), 0) == slip_ref[...])
    spot = iota((16, 16), 0) * 16 + iota((16, 16), 1)
    table = jnp.zeros((16, 16), jnp.float32)
    for (row, system), sign in np.ndenumerate(slip_signs()):
        if sign:
            table = jnp.where(spot == row * 16 + system, float(sign), table)
    signs = jnp.dot(table.astype(jnp.bfloat16), hot, preferred_element_type=jnp.float32)
    factor_ref[...] = signs[:SUB] * np.float32(1 / np.sqrt(6.0))
    blocks, choices = pick_ref.shape
    place = jnp.concatenate([place_ref[...], place_ref[...]], axis=1)
    put = jnp.where(iota((choices, 2 * blocks), 0) == place, 1.0, 0.0)
    put_ref[...] = put.astype(jnp.bfloat16)
    pick_ref[...] = put.T[:blocks].astype(jnp.bfloat16)
    codes = high_ref[...]
    rows = codes.shape[0]
    for c in range(3):
        code_ref[c * rows : (c + 1) * rows, :] = codes * position_ref[c : c + 1, :].astype(jnp.bfloat16)
        code_ref[(3 + c) * rows : (4 + c) * rows, :] = codes * signs[8 + c : 9 + c, :].astype(jnp.bfloat16)
    slots = jnp.dot(code_ref[...], low_ref[...], preferred_element_type=jnp.float32)
    start_ref[...] = slots[: 3 * rows]
    course_ref[...] = slots[3 * rows :] * np.float32(1 / np.sqrt(2.0))


def glide_kernel(order, slabs, *refs):
    pick_ref, mobility_ref, factor_ref, high_ref, low_ref, start_ref, course_ref, weight_ref = refs[:8]
    group = len(order)
    stress_refs = [refs[8 + order.index(k)] for k in range(group)]
    term_ref = refs[8 + group]
    keep_ref, send_ref = refs[9 + group : 11 + group]
    step_ref, move_ref = refs[11 + group :]
    blocks = pick_ref.shape[0]
    held = stress_refs[0].shape[0] // NR
    picked = []
    for c in range(NR):
        stress = jnp.concatenate([ref[c * held : (c + 1) * held, :] for ref in stress_refs], axis=0)
        picked.append(jnp.dot(pick_ref[...], stress, preferred_element_type=jnp.float32))

    span = PACK * SEGB
    mine = iota((PACK, span), 0) == iota((PACK, span), 1) // SEGB
    for g in range(blocks // PACK):
        stress = jnp.concatenate([x[g * PACK : (g + 1) * PACK] for x in picked], axis=0).astype(jnp.bfloat16)
        at = pl.ds(g * span, span)
        sampled = lax.dot_general(stress, weight_ref[at, :], CONTRACT_LANES, preferred_element_type=jnp.float32)
        resolved = sampled[:PACK] * factor_ref[:1, at]
        for c in range(1, NR):
            resolved = resolved + sampled[c * PACK : (c + 1) * PACK] * factor_ref[c : c + 1, at]
        resolved = jnp.sum(jnp.where(mine, resolved, 0.0), axis=0, keepdims=True)
        step = glide_time * mobility_ref[:, at] * resolved
        step_ref[:, at] = step
        term_ref[:, at] = step * factor_ref[:, at]

    step = step_ref[...]
    high = high_ref[...]
    slot_rows = high.shape[0]
    deep = slot_rows // slabs
    step = jnp.dot(high * step.astype(jnp.bfloat16), low_ref[...], preferred_element_type=jnp.float32)
    for c in range(4):
        value = step
        if c < 3:
            at = slice(c * slot_rows, (c + 1) * slot_rows)
            value = start_ref[at, :] + course_ref[at, :] * step
        for t in range(slabs):
            row = ((t % 2 * slabs + t) // 2 * 4 + c) * deep
            move_ref[row : row + deep, :] = value[t * deep : (t + 1) * deep]
    half = keep_ref.shape[0]
    keep_ref[...] = move_ref[:half, :].astype(keep_ref.dtype)
    send_ref[...] = move_ref[half:, :].astype(send_ref.dtype)


def spread_kernel(group, *refs):
    put_ref, term_ref, weight_ref, kept_ref = refs[:4]
    sent_refs = refs[4 : 3 + group]
    blocks = put_ref.shape[1] // 2
    held = kept_ref.shape[0] // NR
    span = PACK * SEGB
    mine = iota((PACK, span), 0) == iota((PACK, span), 1) // SEGB
    parts = []
    for g in range(blocks // PACK):
        at = pl.ds(g * span, span)
        terms = [jnp.where(mine, term_ref[c : c + 1, at], 0.0) for c in range(NR)]
        terms = jnp.concatenate(terms, axis=0).astype(jnp.bfloat16)
        parts.append(jnp.dot(terms, weight_ref[at, :], preferred_element_type=jnp.float32))
    for c in range(NR):
        spread = jnp.concatenate([x[c * PACK : (c + 1) * PACK] for x in parts], axis=0)
        rounded = spread.astype(jnp.bfloat16)
        rest = (spread - rounded.astype(jnp.float32)).astype(jnp.bfloat16)
        dense = jnp.dot(put_ref[...], jnp.concatenate([rounded, rest], axis=0), preferred_element_type=jnp.float32)
        rows = slice(c * held, (c + 1) * held)
        kept_ref[rows, :] = dense[:held]
        for k in range(1, group):
            sent_refs[k - 1][rows, :] = dense[k * held : (k + 1) * held].astype(jnp.bfloat16)


def gather_kernel(chunk, picks, *refs):
    for k, (which, place) in enumerate(picks):
        refs[-1][k * chunk : (k + 1) * chunk, :] = refs[which][place * chunk : (place + 1) * chunk, :]
    rest = len(picks) * chunk
    refs[-1][rest:, :] = jnp.zeros((refs[-1].shape[0] - rest, LANES), refs[-1].dtype)


def total_kernel(*refs):
    kept_ref, got_refs = refs[0], refs[1:-2]
    distortion_ref, sum_ref = refs[-2:]
    total = kept_ref[...]
    for ref in got_refs:
        total = total + ref[...].astype(jnp.float32)
    held = total.shape[0] // NR
    xx, yy, yz, xz, xy = [total[c * held : (c + 1) * held] for c in range(NR)]
    for c, value in enumerate((xx, yy, -(xx + yy), yz, xz, xy)):
        for b in range(0, held, SUB):
            sum_ref[b * NC + c * SUB : b * NC + (c + 1) * SUB, :] = value[b : b + SUB]
    for block in range(held):
        at = slice(block * LANES, (block + 1) * LANES)
        distortion_ref[:, at] = sum_ref[pl.ds(block // SUB * NC * SUB + block % SUB, NC, stride=SUB), :]


def arrive_kernel(slabs, picks, *refs):
    moved_refs = refs[:-2]
    arrived_ref, slot_ref = refs[-2:]
    rows = slot_ref.shape[1]
    deep = rows // 4
    for source, (which, place) in picks.items():
        slot_ref[source] = moved_refs[which][place * rows : (place + 1) * rows, :].astype(jnp.float32)
    me = lax.axis_index("slab")
    for s in range(slabs):
        for b in range(deep):
            lane = (s * deep + b) * LANES
            arrived_ref[:, lane : lane + LANES] = slot_ref[me ^ s, pl.ds(b, 4, stride=deep), :]


def body(
    stress, interp_weight, block_owner, block_local, slip_system, mobility, position, target_slab
):
    group = lax.axis_size("grp")
    slabs = lax.axis_size("slab")
    segments = slip_system.shape[0]
    voxels = stress.shape[1]
    cap = 2 * segments // slabs
    slot_rows = slabs * cap // LANES
    f32, bf16 = jnp.float32, jnp.bfloat16
    shape = jax.ShapeDtypeStruct
    params = pltpu.CompilerParams(vmem_limit_bytes=48 * 1024 * 1024)

    def swap(x, k):
        steps = (k, turned(k, group))
        pairs = [(s * group + g, s * group + (g ^ steps[s % 2])) for s in range(slabs) for g in range(group)]
        return lax.ppermute(x, ("slab", "grp"), pairs)

    peers = sorted(range(1, group), key=lambda k: -bin(k).count("1"))
    blocks = block_local.shape[0]

    def still(x):
        return pltpu.with_memory_space_constraint(x, pltpu.HBM)

    packed, place = pl.pallas_call(
        functools.partial(pack_kernel, group),
        out_shape=(shape((NR * voxels // LANES, LANES), bf16), shape((1, blocks), jnp.int32)),
        in_specs=[HBM] * 3,
        out_specs=[VMEM] * 2,
        scratch_shapes=[
            pltpu.VMEM(stress.shape, bf16),
            pltpu.VMEM((NC * voxels // LANES, LANES), f32),
            pltpu.VMEM((2, 1, blocks), jnp.int32),
            pltpu.SemaphoreType.DMA((3,)),
        ],
        compiler_params=params,
        name="pack",
    )(still(stress), still(block_owner.reshape(1, blocks)), still(block_local.reshape(1, blocks)))
    parts = {k: swap(packed, k) for k in peers}
    parts[0] = packed
    order = [0, *peers]

    slot_shape = (3 * slot_rows, LANES)
    high, low, weight = pl.pallas_call(
        functools.partial(code_kernel, slabs, cap),
        out_shape=(
            shape((slot_rows, segments), bf16),
            shape((segments, LANES), bf16),
            shape((segments, BLK), bf16),
        ),
        in_specs=[VMEM, HBM],
        out_specs=[VMEM] * 3,
        scratch_shapes=[pltpu.SemaphoreType.DMA],
        compiler_params=params,
        name="code",
    )(target_slab.reshape(segments // LANES, LANES), still(interp_weight.reshape(segments, BLK)))
    factor, pick, put, start, course = pl.pallas_call(
        prepare_kernel,
        out_shape=(
            shape((SUB, segments), f32),
            shape((blocks, group * voxels // BLK), bf16),
            shape((group * voxels // BLK, 2 * blocks), bf16),
            shape(slot_shape, f32),
            shape(slot_shape, f32),
        ),
        in_specs=[VMEM] * 5,
        out_specs=[VMEM] * 5,
        scratch_shapes=[pltpu.VMEM((6 * slot_rows, segments), bf16)],
        compiler_params=params,
        name="prepare",
    )(slip_system.reshape(1, segments), place, position, high, low)

    chunk = 4 * slot_rows // slabs
    term, keep, send = pl.pallas_call(
        functools.partial(glide_kernel, order, slabs),
        out_shape=(shape((SUB, segments), f32),) + (shape((slabs // 2 * chunk, LANES), bf16),) * 2,
        in_specs=[VMEM] * (8 + group),
        out_specs=[VMEM] * 3,
        scratch_shapes=[
            pltpu.VMEM((1, segments), f32),
            pltpu.VMEM((4 * slot_rows, LANES), f32),
        ],
        compiler_params=params,
        name="glide",
    )(
        pick,
        mobility.reshape(1, segments),
        factor,
        high,
        low,
        start,
        course,
        weight,
        *[parts[k] for k in order],
    )

    def hop(x, k):
        return lax.ppermute(x, "slab", [(i, i ^ k) for i in range(slabs)])

    arrays = [keep, hop(send, 1)]
    held = {(r, s): (s, r // 2) for r in range(0, slabs, 2) for s in range(2)}
    kept, *sent = pl.pallas_call(
        functools.partial(spread_kernel, group),
        out_shape=(shape(packed.shape, f32),) + (shape(packed.shape, bf16),) * (group - 1),
        in_specs=[VMEM] * 3,
        out_specs=[VMEM] * group,
        compiler_params=params,
        name="spread",
    )(put, term, weight)
    bit = slabs
    while bit > 2:
        bit //= 2
        leaving = {key: at for key, at in sorted(held.items(), key=lambda item: item[0][::-1]) if key[0] & bit}
        through = tuple(sent) if bit == slabs // 2 else ()
        *through, send = pl.pallas_call(
            functools.partial(gather_kernel, chunk, tuple(leaving.values())),
            out_shape=tuple(shape(x.shape, x.dtype) for x in through) + (shape((len(leaving) * chunk + 48, LANES), bf16),),
            in_specs=[VMEM] * (len(arrays) + len(through)),
            out_specs=[VMEM] * (len(through) + 1),
            input_output_aliases={len(arrays) + k: k for k in range(len(through))},
            compiler_params=params,
            name="gather",
        )(*arrays, *through)
        sent = through or sent
        for k, key in enumerate(leaving):
            del held[key]
            held[key[0] ^ bit, key[1] | bit] = (len(arrays), k)
        arrays.append(hop(send, bit))
    got = [swap(sent[k - 1], k) for k in peers]

    distortion = pl.pallas_call(
        total_kernel,
        out_shape=shape((NC, voxels), f32),
        in_specs=[VMEM] * group,
        out_specs=VMEM,
        scratch_shapes=[pltpu.VMEM((NC * voxels // LANES, LANES), f32)],
        compiler_params=params,
        name="total",
    )(kept, *got)
    arrived = pl.pallas_call(
        functools.partial(arrive_kernel, slabs, {s: at for (_, s), at in held.items()}),
        out_shape=shape((4, slabs * cap), f32),
        in_specs=[VMEM] * len(arrays),
        out_specs=VMEM,
        scratch_shapes=[pltpu.VMEM((slabs, chunk, LANES), f32)],
        compiler_params=params,
        name="arrive",
    )(*arrays)
    return (distortion, arrived)


def solution(mesh):
    placed = (
        P(None, ("slab", "grp")),
        P(("slab", "grp"), None, None),
        P(("slab", "grp"), None),
        P(("slab", "grp")),
        P(("slab", "grp")),
        P(("slab", "grp")),
        P(None, ("slab", "grp")),
        P(("slab", "grp"), None),
    )
    return jax.shard_map(
        body,
        mesh=mesh,
        in_specs=placed,
        out_specs=(P(None, ("slab", "grp")), P(None, ("slab", "grp"))),
        check_vma=False,
    )
```

```python
import functools

import jax
import jax.numpy as jnp
import numpy as np
from jax import lax
from jax.experimental import pallas as pl
from jax.experimental.pallas import tpu as pltpu
from jax.sharding import PartitionSpec as P

NC = 6
NR = 5
NSYS = 12
BLK = 128
SEGB = 64
LANES = 128
SUB = 8
PACK = 8

glide_time = 0.5

VMEM = pl.BlockSpec(memory_space=pltpu.VMEM)
HBM = pl.BlockSpec(memory_space=pltpu.HBM)
CONTRACT_LANES = (((1,), (1,)), ((), ()))


def slip_signs():
    normal_list = [(1, 1, 1), (-1, 1, 1), (1, -1, 1), (1, 1, -1)]
    table = np.zeros((16, 16), np.int32)
    system = 0
    for x, y, z in normal_list:
        for burgers in ((y, -x, 0), (z, 0, -x), (0, z, -y)):
            outer = np.outer((x, y, z), burgers)
            tensor = outer + outer.T
            table[:NR, system] = (tensor[0, 0] // 2, tensor[1, 1] // 2, tensor[1, 2], tensor[0, 2], tensor[0, 1])
            table[8:11, system] = burgers
            system += 1
    return table


def iota(shape, dim):
    return lax.broadcasted_iota(jnp.int32, shape, dim)


def mask(condition):
    return jnp.where(condition, 1.0, 0.0).astype(jnp.bfloat16)


def turned(index, group):
    side = group.bit_length() // 2
    return (index & ((1 << side) - 1)) << side | index >> side


def pack_kernel(group, source_ref, owner_ref, local_ref, packed_ref, place_ref, stress_ref, rows_ref, block_ref, sems):
    copies = [
        pltpu.make_async_copy(source_ref, stress_ref, sems.at[0]),
        pltpu.make_async_copy(owner_ref, block_ref.at[0], sems.at[1]),
        pltpu.make_async_copy(local_ref, block_ref.at[1], sems.at[2]),
    ]
    for copy in copies:
        copy.start()
    for copy in copies:
        copy.wait()
    blocks = stress_ref.shape[1] // LANES
    across = block_ref[0] ^ lax.axis_index("grp")
    across = jnp.where(lax.axis_index("slab") % 2 == 1, turned(across, group), across)
    place_ref[...] = across * blocks + block_ref[1]
    for block in range(blocks):
        at = pl.ds(block // SUB * NC * SUB + block % SUB, NC, stride=SUB)
        rows_ref[at, :] = stress_ref[:, block * LANES : (block + 1) * LANES].astype(jnp.float32)

    def component(c):
        pieces = [rows_ref[b * NC + c * SUB : b * NC + (c + 1) * SUB, :] for b in range(0, blocks, SUB)]
        return jnp.concatenate(pieces, axis=0)

    xx, yy, zz, yz, xz, xy = [component(c) for c in range(NC)]
    for c, value in enumerate((xx - zz, yy - zz, yz, xz, xy)):
        packed_ref[c * blocks : (c + 1) * blocks, :] = value.astype(jnp.bfloat16)


def code_kernel(slabs, cap, target_ref, source_ref, high_ref, low_ref, weight_ref, across_ref, sem):
    fetch = pltpu.make_async_copy(source_ref, weight_ref, sem)
    fetch.start()
    chunks = target_ref.shape[0]
    target = target_ref[...] ^ lax.axis_index("slab")
    upto = mask(iota((LANES, LANES), 0) <= iota((LANES, LANES), 1))
    ones = jnp.ones((LANES, LANES), jnp.bfloat16)
    before = mask(iota((chunks, chunks), 1) < iota((chunks, chunks), 0))
    slot = target * cap
    for t in range(slabs):
        here = mask(target == t)
        inside = jnp.dot(here, upto, preferred_element_type=jnp.float32)
        total = jnp.dot(here, ones, preferred_element_type=jnp.float32)
        ahead = jnp.dot(before, total.astype(jnp.bfloat16), preferred_element_type=jnp.float32)
        rank = (inside + ahead).astype(jnp.int32) - 1
        slot = slot + jnp.where(target == t, rank, 0)
    high = slot // LANES
    low = (slot % LANES).T
    rows = slabs * cap // LANES
    for r in range(chunks):
        at = pl.ds(r * LANES, LANES)
        high_ref[:, at] = mask(iota((rows, LANES), 0) == high[r : r + 1, :])
        low_ref[at, :] = mask(iota((LANES, LANES), 1) == low[:, r : r + 1])
    fetch.wait()
    unit = mask(iota((LANES, LANES), 0) == iota((LANES, LANES), 1))
    span = PACK * SEGB
    for g in range(weight_ref.shape[0] // span):
        at = pl.ds(g * span, span)
        turn = lax.dot_general(unit, weight_ref[at, :], CONTRACT_LANES, preferred_element_type=jnp.float32)
        across_ref[:, at] = turn.astype(jnp.bfloat16)


def prepare_kernel(*refs):
    slip_ref, place_ref, position_ref, high_ref, low_ref = refs[:5]
    factor_ref, pick_ref, put_ref, start_ref, course_ref, code_ref = refs[5:]
    segments = slip_ref.shape[1]
    hot = mask(iota((16, segments), 0) == slip_ref[...])
    spot = iota((16, 16), 0) * 16 + iota((16, 16), 1)
    table = jnp.zeros((16, 16), jnp.float32)
    for (row, system), sign in np.ndenumerate(slip_signs()):
        if sign:
            table = jnp.where(spot == row * 16 + system, float(sign), table)
    signs = jnp.dot(table.astype(jnp.bfloat16), hot, preferred_element_type=jnp.float32)
    factor_ref[...] = signs[:SUB] * np.float32(1 / np.sqrt(6.0))
    blocks, choices = pick_ref.shape
    place = jnp.concatenate([place_ref[...], place_ref[...]], axis=1)
    put = jnp.where(iota((choices, 2 * blocks), 0) == place, 1.0, 0.0)
    put_ref[...] = put.astype(jnp.bfloat16)
    pick_ref[...] = put.T[:blocks].astype(jnp.bfloat16)
    codes = high_ref[...]
    rows = codes.shape[0]
    for c in range(3):
        code_ref[c * rows : (c + 1) * rows, :] = codes * position_ref[c : c + 1, :].astype(jnp.bfloat16)
        code_ref[(3 + c) * rows : (4 + c) * rows, :] = codes * signs[8 + c : 9 + c, :].astype(jnp.bfloat16)
    slots = jnp.dot(code_ref[...], low_ref[...], preferred_element_type=jnp.float32)
    start_ref[...] = slots[: 3 * rows]
    course_ref[...] = slots[3 * rows :] * np.float32(1 / np.sqrt(2.0))


def glide_kernel(order, slabs, *refs):
    pick_ref, mobility_ref, factor_ref, high_ref, low_ref, start_ref, course_ref, across_ref = refs[:8]
    group = len(order)
    stress_refs = [refs[8 + order.index(k)] for k in range(group)]
    term_ref = refs[8 + group]
    keep_ref, send_ref = refs[9 + group : 11 + group]
    step_ref, move_ref = refs[11 + group :]
    blocks = pick_ref.shape[0]
    held = stress_refs[0].shape[0] // NR
    picked = []
    for c in range(NR):
        stress = jnp.concatenate([ref[c * held : (c + 1) * held, :] for ref in stress_refs], axis=0)
        picked.append(jnp.dot(pick_ref[...], stress, preferred_element_type=jnp.float32))

    span = PACK * SEGB
    mine = iota((PACK, span), 0) == iota((PACK, span), 1) // SEGB
    for g in range(blocks // PACK):
        stress = jnp.concatenate([x[g * PACK : (g + 1) * PACK] for x in picked], axis=0).astype(jnp.bfloat16)
        at = pl.ds(g * span, span)
        sampled = jnp.dot(stress, across_ref[:, at], preferred_element_type=jnp.float32)
        resolved = sampled[:PACK] * factor_ref[:1, at]
        for c in range(1, NR):
            resolved = resolved + sampled[c * PACK : (c + 1) * PACK] * factor_ref[c : c + 1, at]
        resolved = jnp.sum(jnp.where(mine, resolved, 0.0), axis=0, keepdims=True)
        step = glide_time * mobility_ref[:, at] * resolved
        step_ref[:, at] = step
        term_ref[:, at] = step * factor_ref[:, at]

    step = step_ref[...]
    high = high_ref[...]
    slot_rows = high.shape[0]
    deep = slot_rows // slabs
    step = jnp.dot(high * step.astype(jnp.bfloat16), low_ref[...], preferred_element_type=jnp.float32)
    for c in range(4):
        value = step
        if c < 3:
            at = slice(c * slot_rows, (c + 1) * slot_rows)
            value = start_ref[at, :] + course_ref[at, :] * step
        for t in range(slabs):
            row = ((t % 2 * slabs + t) // 2 * 4 + c) * deep
            move_ref[row : row + deep, :] = value[t * deep : (t + 1) * deep]
    half = keep_ref.shape[0]
    keep_ref[...] = move_ref[:half, :].astype(keep_ref.dtype)
    send_ref[...] = move_ref[half:, :].astype(send_ref.dtype)


def spread_kernel(group, *refs):
    put_ref, term_ref, weight_ref, kept_ref = refs[:4]
    sent_refs = refs[4 : 3 + group]
    blocks = put_ref.shape[1] // 2
    held = kept_ref.shape[0] // NR
    span = PACK * SEGB
    mine = iota((PACK, span), 0) == iota((PACK, span), 1) // SEGB
    parts = []
    for g in range(blocks // PACK):
        at = pl.ds(g * span, span)
        terms = [jnp.where(mine, term_ref[c : c + 1, at], 0.0) for c in range(NR)]
        terms = jnp.concatenate(terms, axis=0).astype(jnp.bfloat16)
        parts.append(jnp.dot(terms, weight_ref[at, :], preferred_element_type=jnp.float32))
    for c in range(NR):
        spread = jnp.concatenate([x[c * PACK : (c + 1) * PACK] for x in parts], axis=0)
        rounded = spread.astype(jnp.bfloat16)
        rest = (spread - rounded.astype(jnp.float32)).astype(jnp.bfloat16)
        dense = jnp.dot(put_ref[...], jnp.concatenate([rounded, rest], axis=0), preferred_element_type=jnp.float32)
        rows = slice(c * held, (c + 1) * held)
        kept_ref[rows, :] = dense[:held]
        for k in range(1, group):
            sent_refs[k - 1][rows, :] = dense[k * held : (k + 1) * held].astype(jnp.bfloat16)


def gather_kernel(chunk, picks, *refs):
    for k, (which, place) in enumerate(picks):
        refs[-1][k * chunk : (k + 1) * chunk, :] = refs[which][place * chunk : (place + 1) * chunk, :]
    rest = len(picks) * chunk
    refs[-1][rest:, :] = jnp.zeros((refs[-1].shape[0] - rest, LANES), refs[-1].dtype)


def total_kernel(*refs):
    kept_ref, got_refs = refs[0], refs[1:-2]
    distortion_ref, sum_ref = refs[-2:]
    total = kept_ref[...]
    for ref in got_refs:
        total = total + ref[...].astype(jnp.float32)
    held = total.shape[0] // NR
    xx, yy, yz, xz, xy = [total[c * held : (c + 1) * held] for c in range(NR)]
    for c, value in enumerate((xx, yy, -(xx + yy), yz, xz, xy)):
        for b in range(0, held, SUB):
            sum_ref[b * NC + c * SUB : b * NC + (c + 1) * SUB, :] = value[b : b + SUB]
    for block in range(held):
        at = slice(block * LANES, (block + 1) * LANES)
        distortion_ref[:, at] = sum_ref[pl.ds(block // SUB * NC * SUB + block % SUB, NC, stride=SUB), :]


def arrive_kernel(slabs, picks, *refs):
    moved_refs = refs[:-2]
    arrived_ref, slot_ref = refs[-2:]
    rows = slot_ref.shape[1]
    deep = rows // 4
    for source, (which, place) in picks.items():
        slot_ref[source] = moved_refs[which][place * rows : (place + 1) * rows, :].astype(jnp.float32)
    me = lax.axis_index("slab")
    for s in range(slabs):
        for b in range(deep):
            lane = (s * deep + b) * LANES
            arrived_ref[:, lane : lane + LANES] = slot_ref[me ^ s, pl.ds(b, 4, stride=deep), :]


def body(
    stress, interp_weight, block_owner, block_local, slip_system, mobility, position, target_slab
):
    group = lax.axis_size("grp")
    slabs = lax.axis_size("slab")
    segments = slip_system.shape[0]
    voxels = stress.shape[1]
    cap = 2 * segments // slabs
    slot_rows = slabs * cap // LANES
    f32, bf16 = jnp.float32, jnp.bfloat16
    shape = jax.ShapeDtypeStruct
    params = pltpu.CompilerParams(vmem_limit_bytes=48 * 1024 * 1024)

    def swap(x, k):
        steps = (k, turned(k, group))
        pairs = [(s * group + g, s * group + (g ^ steps[s % 2])) for s in range(slabs) for g in range(group)]
        return lax.ppermute(x, ("slab", "grp"), pairs)

    peers = sorted(range(1, group), key=lambda k: -bin(k).count("1"))
    blocks = block_local.shape[0]

    def still(x):
        return pltpu.with_memory_space_constraint(x, pltpu.HBM)

    packed, place = pl.pallas_call(
        functools.partial(pack_kernel, group),
        out_shape=(shape((NR * voxels // LANES, LANES), bf16), shape((1, blocks), jnp.int32)),
        in_specs=[HBM] * 3,
        out_specs=[VMEM] * 2,
        scratch_shapes=[
            pltpu.VMEM(stress.shape, bf16),
            pltpu.VMEM((NC * voxels // LANES, LANES), f32),
            pltpu.VMEM((2, 1, blocks), jnp.int32),
            pltpu.SemaphoreType.DMA((3,)),
        ],
        compiler_params=params,
        name="pack",
    )(still(stress), still(block_owner.reshape(1, blocks)), still(block_local.reshape(1, blocks)))
    parts = {k: swap(packed, k) for k in peers}
    parts[0] = packed
    order = [0, *peers[::-1]]

    slot_shape = (3 * slot_rows, LANES)
    high, low, weight, weight_across = pl.pallas_call(
        functools.partial(code_kernel, slabs, cap),
        out_shape=(
            shape((slot_rows, segments), bf16),
            shape((segments, LANES), bf16),
            shape((segments, BLK), bf16),
            shape((BLK, segments), bf16),
        ),
        in_specs=[VMEM, HBM],
        out_specs=[VMEM] * 4,
        scratch_shapes=[pltpu.SemaphoreType.DMA],
        compiler_params=params,
        name="code",
    )(target_slab.reshape(segments // LANES, LANES), still(interp_weight.reshape(segments, BLK)))
    factor, pick, put, start, course = pl.pallas_call(
        prepare_kernel,
        out_shape=(
            shape((SUB, segments), f32),
            shape((blocks, group * voxels // BLK), bf16),
            shape((group * voxels // BLK, 2 * blocks), bf16),
            shape(slot_shape, f32),
            shape(slot_shape, f32),
        ),
        in_specs=[VMEM] * 5,
        out_specs=[VMEM] * 5,
        scratch_shapes=[pltpu.VMEM((6 * slot_rows, segments), bf16)],
        compiler_params=params,
        name="prepare",
    )(slip_system.reshape(1, segments), place, position, high, low)

    chunk = 4 * slot_rows // slabs
    term, keep, send = pl.pallas_call(
        functools.partial(glide_kernel, order, slabs),
        out_shape=(shape((SUB, segments), f32),) + (shape((slabs // 2 * chunk, LANES), bf16),) * 2,
        in_specs=[VMEM] * (8 + group),
        out_specs=[VMEM] * 3,
        scratch_shapes=[
            pltpu.VMEM((1, segments), f32),
            pltpu.VMEM((4 * slot_rows, LANES), f32),
        ],
        compiler_params=params,
        name="glide",
    )(
        pick,
        mobility.reshape(1, segments),
        factor,
        high,
        low,
        start,
        course,
        weight_across,
        *[parts[k] for k in order],
    )

    def hop(x, k):
        return lax.ppermute(x, "slab", [(i, i ^ k) for i in range(slabs)])

    arrays = [keep, hop(send, 1)]
    held = {(r, s): (s, r // 2) for r in range(0, slabs, 2) for s in range(2)}
    kept, *sent = pl.pallas_call(
        functools.partial(spread_kernel, group),
        out_shape=(shape(packed.shape, f32),) + (shape(packed.shape, bf16),) * (group - 1),
        in_specs=[VMEM] * 3,
        out_specs=[VMEM] * group,
        compiler_params=params,
        name="spread",
    )(put, term, weight)
    bit = slabs
    while bit > 2:
        bit //= 2
        leaving = {key: at for key, at in sorted(held.items(), key=lambda item: item[0][::-1]) if key[0] & bit}
        through = tuple(sent) if bit == slabs // 2 else ()
        *through, send = pl.pallas_call(
            functools.partial(gather_kernel, chunk, tuple(leaving.values())),
            out_shape=tuple(shape(x.shape, x.dtype) for x in through) + (shape((len(leaving) * chunk + 48, LANES), bf16),),
            in_specs=[VMEM] * (len(arrays) + len(through)),
            out_specs=[VMEM] * (len(through) + 1),
            input_output_aliases={len(arrays) + k: k for k in range(len(through))},
            compiler_params=params,
            name="gather",
        )(*arrays, *through)
        sent = through or sent
        for k, key in enumerate(leaving):
            del held[key]
            held[key[0] ^ bit, key[1] | bit] = (len(arrays), k)
        arrays.append(hop(send, bit))
    got = [swap(sent[k - 1], k) for k in peers]

    distortion = pl.pallas_call(
        total_kernel,
        out_shape=shape((NC, voxels), f32),
        in_specs=[VMEM] * group,
        out_specs=VMEM,
        scratch_shapes=[pltpu.VMEM((NC * voxels // LANES, LANES), f32)],
        compiler_params=params,
        name="total",
    )(kept, *got)
    arrived = pl.pallas_call(
        functools.partial(arrive_kernel, slabs, {s: at for (_, s), at in held.items()}),
        out_shape=shape((4, slabs * cap), f32),
        in_specs=[VMEM] * len(arrays),
        out_specs=VMEM,
        scratch_shapes=[pltpu.VMEM((slabs, chunk, LANES), f32)],
        compiler_params=params,
        name="arrive",
    )(*arrays)
    return (distortion, arrived)


def solution(mesh):
    placed = (
        P(None, ("slab", "grp")),
        P(("slab", "grp"), None, None),
        P(("slab", "grp"), None),
        P(("slab", "grp")),
        P(("slab", "grp")),
        P(("slab", "grp")),
        P(None, ("slab", "grp")),
        P(("slab", "grp"), None),
    )
    return jax.shard_map(
        body,
        mesh=mesh,
        in_specs=placed,
        out_specs=(P(None, ("slab", "grp")), P(None, ("slab", "grp"))),
        check_vma=False,
    )
```

```python
import functools

import jax
import jax.numpy as jnp
import numpy as np
from jax import lax
from jax.experimental import pallas as pl
from jax.experimental.pallas import tpu as pltpu
from jax.sharding import PartitionSpec as P

NC = 6
NR = 5
NSYS = 12
BLK = 128
SEGB = 64
LANES = 128
SUB = 8
PACK = 8

glide_time = 0.5

VMEM = pl.BlockSpec(memory_space=pltpu.VMEM)
HBM = pl.BlockSpec(memory_space=pltpu.HBM)
CONTRACT_LANES = (((1,), (1,)), ((), ()))


def slip_signs():
    normal_list = [(1, 1, 1), (-1, 1, 1), (1, -1, 1), (1, 1, -1)]
    table = np.zeros((16, 16), np.int32)
    system = 0
    for x, y, z in normal_list:
        for burgers in ((y, -x, 0), (z, 0, -x), (0, z, -y)):
            outer = np.outer((x, y, z), burgers)
            tensor = outer + outer.T
            table[:NR, system] = (tensor[0, 0] // 2, tensor[1, 1] // 2, tensor[1, 2], tensor[0, 2], tensor[0, 1])
            table[8:11, system] = burgers
            system += 1
    return table


def iota(shape, dim):
    return lax.broadcasted_iota(jnp.int32, shape, dim)


def mask(condition):
    return jnp.where(condition, 1.0, 0.0).astype(jnp.bfloat16)


def turned(index, group):
    side = group.bit_length() // 2
    return (index & ((1 << side) - 1)) << side | index >> side


def pack_kernel(group, source_ref, owner_ref, local_ref, packed_ref, place_ref, stress_ref, rows_ref, block_ref, sems):
    copies = [
        pltpu.make_async_copy(source_ref, stress_ref, sems.at[0]),
        pltpu.make_async_copy(owner_ref, block_ref.at[0], sems.at[1]),
        pltpu.make_async_copy(local_ref, block_ref.at[1], sems.at[2]),
    ]
    for copy in copies:
        copy.start()
    for copy in copies:
        copy.wait()
    blocks = stress_ref.shape[1] // LANES
    across = block_ref[0] ^ lax.axis_index("grp")
    across = jnp.where(lax.axis_index("slab") % 2 == 1, turned(across, group), across)
    place_ref[...] = across * blocks + block_ref[1]
    for block in range(blocks):
        at = pl.ds(block // SUB * NC * SUB + block % SUB, NC, stride=SUB)
        rows_ref[at, :] = stress_ref[:, block * LANES : (block + 1) * LANES].astype(jnp.float32)

    def component(c):
        pieces = [rows_ref[b * NC + c * SUB : b * NC + (c + 1) * SUB, :] for b in range(0, blocks, SUB)]
        return jnp.concatenate(pieces, axis=0)

    xx, yy, zz, yz, xz, xy = [component(c) for c in range(NC)]
    for c, value in enumerate((xx - zz, yy - zz, yz, xz, xy)):
        packed_ref[c * blocks : (c + 1) * blocks, :] = value.astype(jnp.bfloat16)


def code_kernel(slabs, cap, target_ref, source_ref, high_ref, low_ref, weight_ref, across_ref, sem):
    fetch = pltpu.make_async_copy(source_ref, weight_ref, sem)
    fetch.start()
    chunks = target_ref.shape[0]
    target = target_ref[...] ^ lax.axis_index("slab")
    upto = mask(iota((LANES, LANES), 0) <= iota((LANES, LANES), 1))
    ones = jnp.ones((LANES, LANES), jnp.bfloat16)
    before = mask(iota((chunks, chunks), 1) < iota((chunks, chunks), 0))
    slot = target * cap
    for t in range(slabs):
        here = mask(target == t)
        inside = jnp.dot(here, upto, preferred_element_type=jnp.float32)
        total = jnp.dot(here, ones, preferred_element_type=jnp.float32)
        ahead = jnp.dot(before, total.astype(jnp.bfloat16), preferred_element_type=jnp.float32)
        rank = (inside + ahead).astype(jnp.int32) - 1
        slot = slot + jnp.where(target == t, rank, 0)
    high = slot // LANES
    low = (slot % LANES).T
    rows = slabs * cap // LANES
    for r in range(chunks):
        at = pl.ds(r * LANES, LANES)
        high_ref[:, at] = mask(iota((rows, LANES), 0) == high[r : r + 1, :])
        low_ref[at, :] = mask(iota((LANES, LANES), 1) == low[:, r : r + 1])
    fetch.wait()
    unit = mask(iota((LANES, LANES), 0) == iota((LANES, LANES), 1))
    span = PACK * SEGB
    for g in range(weight_ref.shape[0] // span):
        at = pl.ds(g * span, span)
        turn = lax.dot_general(unit, weight_ref[at, :], CONTRACT_LANES, preferred_element_type=jnp.float32)
        across_ref[:, at] = turn.astype(jnp.bfloat16)


def prepare_kernel(*refs):
    slip_ref, place_ref, position_ref, high_ref, low_ref = refs[:5]
    factor_ref, pick_ref, put_ref, start_ref, course_ref, code_ref = refs[5:]
    segments = slip_ref.shape[1]
    hot = mask(iota((16, segments), 0) == slip_ref[...])
    spot = iota((16, 16), 0) * 16 + iota((16, 16), 1)
    table = jnp.zeros((16, 16), jnp.float32)
    for (row, system), sign in np.ndenumerate(slip_signs()):
        if sign:
            table = jnp.where(spot == row * 16 + system, float(sign), table)
    signs = jnp.dot(table.astype(jnp.bfloat16), hot, preferred_element_type=jnp.float32)
    factor_ref[...] = signs[:SUB] * np.float32(1 / np.sqrt(6.0))
    blocks, choices = pick_ref.shape
    place = jnp.concatenate([place_ref[...], place_ref[...]], axis=1)
    put = jnp.where(iota((choices, 2 * blocks), 0) == place, 1.0, 0.0)
    put_ref[...] = put.astype(jnp.bfloat16)
    pick_ref[...] = put.T[:blocks].astype(jnp.bfloat16)
    codes = high_ref[...]
    rows = codes.shape[0]
    for c in range(3):
        code_ref[c * rows : (c + 1) * rows, :] = codes * position_ref[c : c + 1, :].astype(jnp.bfloat16)
        code_ref[(3 + c) * rows : (4 + c) * rows, :] = codes * signs[8 + c : 9 + c, :].astype(jnp.bfloat16)
    slots = jnp.dot(code_ref[...], low_ref[...], preferred_element_type=jnp.float32)
    start_ref[...] = slots[: 3 * rows]
    course_ref[...] = slots[3 * rows :] * np.float32(1 / np.sqrt(2.0))


def glide_kernel(order, slabs, *refs):
    pick_ref, mobility_ref, factor_ref, high_ref, low_ref, start_ref, course_ref, across_ref = refs[:8]
    group = len(order)
    stress_refs = [refs[8 + order.index(k)] for k in range(group)]
    step_ref, keep_ref, send_ref, move_ref = refs[8 + group :]
    blocks = pick_ref.shape[0]
    held = stress_refs[0].shape[0] // NR
    picked = []
    for c in range(NR):
        stress = jnp.concatenate([ref[c * held : (c + 1) * held, :] for ref in stress_refs], axis=0)
        picked.append(jnp.dot(pick_ref[...], stress, preferred_element_type=jnp.float32))

    span = PACK * SEGB
    mine = iota((PACK, span), 0) == iota((PACK, span), 1) // SEGB
    for g in range(blocks // PACK):
        stress = jnp.concatenate([x[g * PACK : (g + 1) * PACK] for x in picked], axis=0).astype(jnp.bfloat16)
        at = pl.ds(g * span, span)
        sampled = jnp.dot(stress, across_ref[:, at], preferred_element_type=jnp.float32)
        resolved = sampled[:PACK] * factor_ref[:1, at]
        for c in range(1, NR):
            resolved = resolved + sampled[c * PACK : (c + 1) * PACK] * factor_ref[c : c + 1, at]
        resolved = jnp.sum(jnp.where(mine, resolved, 0.0), axis=0, keepdims=True)
        step = glide_time * mobility_ref[:, at] * resolved
        step_ref[:, at] = step

    step = step_ref[...]
    high = high_ref[...]
    slot_rows = high.shape[0]
    deep = slot_rows // slabs
    step = jnp.dot(high * step.astype(jnp.bfloat16), low_ref[...], preferred_element_type=jnp.float32)
    for c in range(4):
        value = step
        if c < 3:
            at = slice(c * slot_rows, (c + 1) * slot_rows)
            value = start_ref[at, :] + course_ref[at, :] * step
        for t in range(slabs):
            row = ((t % 2 * slabs + t) // 2 * 4 + c) * deep
            move_ref[row : row + deep, :] = value[t * deep : (t + 1) * deep]
    half = keep_ref.shape[0]
    keep_ref[...] = move_ref[:half, :].astype(keep_ref.dtype)
    send_ref[...] = move_ref[half:, :].astype(send_ref.dtype)


def spread_kernel(group, *refs):
    put_ref, step_ref, factor_ref, weight_ref, kept_ref = refs[:5]
    sent_refs = refs[5:]
    blocks = put_ref.shape[1] // 2
    held = kept_ref.shape[0] // NR
    span = PACK * SEGB
    mine = iota((PACK, span), 0) == iota((PACK, span), 1) // SEGB
    parts = []
    for g in range(blocks // PACK):
        at = pl.ds(g * span, span)
        terms = [jnp.where(mine, step_ref[:, at] * factor_ref[c : c + 1, at], 0.0) for c in range(NR)]
        terms = jnp.concatenate(terms, axis=0).astype(jnp.bfloat16)
        parts.append(jnp.dot(terms, weight_ref[at, :], preferred_element_type=jnp.float32))
    for c in range(NR):
        spread = jnp.concatenate([x[c * PACK : (c + 1) * PACK] for x in parts], axis=0)
        rounded = spread.astype(jnp.bfloat16)
        rest = (spread - rounded.astype(jnp.float32)).astype(jnp.bfloat16)
        dense = jnp.dot(put_ref[...], jnp.concatenate([rounded, rest], axis=0), preferred_element_type=jnp.float32)
        rows = slice(c * held, (c + 1) * held)
        kept_ref[rows, :] = dense[:held]
        for k in range(1, group):
            sent_refs[k - 1][rows, :] = dense[k * held : (k + 1) * held].astype(jnp.bfloat16)


def gather_kernel(chunk, picks, *refs):
    for k, (which, place) in enumerate(picks):
        refs[-1][k * chunk : (k + 1) * chunk, :] = refs[which][place * chunk : (place + 1) * chunk, :]
    rest = len(picks) * chunk
    refs[-1][rest:, :] = jnp.zeros((refs[-1].shape[0] - rest, LANES), refs[-1].dtype)


def total_kernel(*refs):
    kept_ref, got_refs = refs[0], refs[1:-2]
    distortion_ref, sum_ref = refs[-2:]
    total = kept_ref[...]
    for ref in got_refs:
        total = total + ref[...].astype(jnp.float32)
    held = total.shape[0] // NR
    xx, yy, yz, xz, xy = [total[c * held : (c + 1) * held] for c in range(NR)]
    for c, value in enumerate((xx, yy, -(xx + yy), yz, xz, xy)):
        for b in range(0, held, SUB):
            sum_ref[b * NC + c * SUB : b * NC + (c + 1) * SUB, :] = value[b : b + SUB]
    for block in range(held):
        at = slice(block * LANES, (block + 1) * LANES)
        distortion_ref[:, at] = sum_ref[pl.ds(block // SUB * NC * SUB + block % SUB, NC, stride=SUB), :]


def arrive_kernel(slabs, picks, *refs):
    moved_refs = refs[:-2]
    arrived_ref, slot_ref = refs[-2:]
    rows = slot_ref.shape[1]
    deep = rows // 4
    for source, (which, place) in picks.items():
        slot_ref[source] = moved_refs[which][place * rows : (place + 1) * rows, :].astype(jnp.float32)
    me = lax.axis_index("slab")
    for s in range(slabs):
        for b in range(deep):
            lane = (s * deep + b) * LANES
            arrived_ref[:, lane : lane + LANES] = slot_ref[me ^ s, pl.ds(b, 4, stride=deep), :]


def body(
    stress, interp_weight, block_owner, block_local, slip_system, mobility, position, target_slab
):
    group = lax.axis_size("grp")
    slabs = lax.axis_size("slab")
    segments = slip_system.shape[0]
    voxels = stress.shape[1]
    cap = 2 * segments // slabs
    slot_rows = slabs * cap // LANES
    f32, bf16 = jnp.float32, jnp.bfloat16
    shape = jax.ShapeDtypeStruct
    params = pltpu.CompilerParams(vmem_limit_bytes=48 * 1024 * 1024)

    def swap(x, k):
        steps = (k, turned(k, group))
        pairs = [(s * group + g, s * group + (g ^ steps[s % 2])) for s in range(slabs) for g in range(group)]
        return lax.ppermute(x, ("slab", "grp"), pairs)

    peers = sorted(range(1, group), key=lambda k: -bin(k).count("1"))
    blocks = block_local.shape[0]

    def still(x):
        return pltpu.with_memory_space_constraint(x, pltpu.HBM)

    packed, place = pl.pallas_call(
        functools.partial(pack_kernel, group),
        out_shape=(shape((NR * voxels // LANES, LANES), bf16), shape((1, blocks), jnp.int32)),
        in_specs=[HBM] * 3,
        out_specs=[VMEM] * 2,
        scratch_shapes=[
            pltpu.VMEM(stress.shape, bf16),
            pltpu.VMEM((NC * voxels // LANES, LANES), f32),
            pltpu.VMEM((2, 1, blocks), jnp.int32),
            pltpu.SemaphoreType.DMA((3,)),
        ],
        compiler_params=params,
        name="pack",
    )(still(stress), still(block_owner.reshape(1, blocks)), still(block_local.reshape(1, blocks)))
    parts = {k: swap(packed, k) for k in peers}
    parts[0] = packed
    order = [0, *peers[::-1]]

    slot_shape = (3 * slot_rows, LANES)
    high, low, weight, weight_across = pl.pallas_call(
        functools.partial(code_kernel, slabs, cap),
        out_shape=(
            shape((slot_rows, segments), bf16),
            shape((segments, LANES), bf16),
            shape((segments, BLK), bf16),
            shape((BLK, segments), bf16),
        ),
        in_specs=[VMEM, HBM],
        out_specs=[VMEM] * 4,
        scratch_shapes=[pltpu.SemaphoreType.DMA],
        compiler_params=params,
        name="code",
    )(target_slab.reshape(segments // LANES, LANES), still(interp_weight.reshape(segments, BLK)))
    factor, pick, put, start, course = pl.pallas_call(
        prepare_kernel,
        out_shape=(
            shape((SUB, segments), f32),
            shape((blocks, group * voxels // BLK), bf16),
            shape((group * voxels // BLK, 2 * blocks), bf16),
            shape(slot_shape, f32),
            shape(slot_shape, f32),
        ),
        in_specs=[VMEM] * 5,
        out_specs=[VMEM] * 5,
        scratch_shapes=[pltpu.VMEM((6 * slot_rows, segments), bf16)],
        compiler_params=params,
        name="prepare",
    )(slip_system.reshape(1, segments), place, position, high, low)

    chunk = 4 * slot_rows // slabs
    step, keep, send = pl.pallas_call(
        functools.partial(glide_kernel, order, slabs),
        out_shape=(shape((1, segments), f32),) + (shape((slabs // 2 * chunk, LANES), bf16),) * 2,
        in_specs=[VMEM] * (8 + group),
        out_specs=[VMEM] * 3,
        scratch_shapes=[pltpu.VMEM((4 * slot_rows, LANES), f32)],
        compiler_params=params,
        name="glide",
    )(
        pick,
        mobility.reshape(1, segments),
        factor,
        high,
        low,
        start,
        course,
        weight_across,
        *[parts[k] for k in order],
    )

    def hop(x, k):
        return lax.ppermute(x, "slab", [(i, i ^ k) for i in range(slabs)])

    arrays = [keep, hop(send, 1)]
    held = {(r, s): (s, r // 2) for r in range(0, slabs, 2) for s in range(2)}
    kept, *sent = pl.pallas_call(
        functools.partial(spread_kernel, group),
        out_shape=(shape(packed.shape, f32),) + (shape(packed.shape, bf16),) * (group - 1),
        in_specs=[VMEM] * 4,
        out_specs=[VMEM] * group,
        compiler_params=params,
        name="spread",
    )(put, step, factor, weight)
    bit = slabs
    while bit > 2:
        bit //= 2
        leaving = {key: at for key, at in sorted(held.items(), key=lambda item: item[0][::-1]) if key[0] & bit}
        through = tuple(sent) if bit == slabs // 2 else ()
        *through, send = pl.pallas_call(
            functools.partial(gather_kernel, chunk, tuple(leaving.values())),
            out_shape=tuple(shape(x.shape, x.dtype) for x in through) + (shape((len(leaving) * chunk + 48, LANES), bf16),),
            in_specs=[VMEM] * (len(arrays) + len(through)),
            out_specs=[VMEM] * (len(through) + 1),
            input_output_aliases={len(arrays) + k: k for k in range(len(through))},
            compiler_params=params,
            name="gather",
        )(*arrays, *through)
        sent = through or sent
        for k, key in enumerate(leaving):
            del held[key]
            held[key[0] ^ bit, key[1] | bit] = (len(arrays), k)
        arrays.append(hop(send, bit))
    got = [swap(sent[k - 1], k) for k in peers]

    distortion = pl.pallas_call(
        total_kernel,
        out_shape=shape((NC, voxels), f32),
        in_specs=[VMEM] * group,
        out_specs=VMEM,
        scratch_shapes=[pltpu.VMEM((NC * voxels // LANES, LANES), f32)],
        compiler_params=params,
        name="total",
    )(kept, *got)
    arrived = pl.pallas_call(
        functools.partial(arrive_kernel, slabs, {s: at for (_, s), at in held.items()}),
        out_shape=shape((4, slabs * cap), f32),
        in_specs=[VMEM] * len(arrays),
        out_specs=VMEM,
        scratch_shapes=[pltpu.VMEM((slabs, chunk, LANES), f32)],
        compiler_params=params,
        name="arrive",
    )(*arrays)
    return (distortion, arrived)


def solution(mesh):
    placed = (
        P(None, ("slab", "grp")),
        P(("slab", "grp"), None, None),
        P(("slab", "grp"), None),
        P(("slab", "grp")),
        P(("slab", "grp")),
        P(("slab", "grp")),
        P(None, ("slab", "grp")),
        P(("slab", "grp"), None),
    )
    return jax.shard_map(
        body,
        mesh=mesh,
        in_specs=placed,
        out_specs=(P(None, ("slab", "grp")), P(None, ("slab", "grp"))),
        check_vma=False,
    )
```
